1024 devices in a mesh: gx: 16 (over x, z_hi), gy: 8 (over y), gz: 8 (over z_lo, core).
Axes of the slice: x: 4, y: 8, z: 16 (z_hi: 4, z_lo: 4; z = z_hi * 4 + z_lo), core: 2. Of those that a mesh axis runs over, the one named last changes fastest.
Arguments:
- right_side: float32 [3, 512, 32768], P(None, None, ('gx', 'gy', 'gz')), may hold values from -6 to 6
- geometry: float32 [6, 128, 128, 1024], P(None, 'gx', 'gy', 'gz'), may hold values from -1.4 to 4, as said below
- viscosity: float32 [128, 128, 1024], P('gx', 'gy', 'gz'), may hold values from 0.3 to 3
- eig_low: float32 [1], replicated, may hold values from 0.2 to 2
- eig_high: float32 [1], replicated, may hold values from 8 to 12
- element_slot: int32 [1024, 32], P(('gx', 'gy', 'gz')), may hold values from 0 to 31, each once within a row
- dirichlet: int32 [2, 3, 128, 1024], P(None, None, 'gy', 'gz'), may hold values 0 or 1
Outputs:
- solution_field: float32 [3, 512, 32768], P(None, None, ('gx', 'gy', 'gz'))
The draws below stay inside these ranges and needn't reach their ends.
Inputs may be any that keep to these rules, and one draw needn't show every extreme that they name: `element_slot`: each row holds each number from 0 to 31 once. `geometry`: the six entries of each node, in the order xx, yy, zz, xy, xz, yz, form a symmetric positive definite matrix.
All inputs are finite; a program needn't handle non-finite values. No bound on the sum of `dirichlet` on one device may be relied on, other than what follows from the above.
Results may differ from the reference program's by a relative error of at most 0.0003.
Values sent between devices are 32-bit elements; how exact they have to be, the bound alone decides.
A program may use at most 32 MiB of HBM per device.

```python
import math
import jax
import jax.numpy as jnp
import numpy as np
from jax import lax

DEGREE = 7
COMPS = 3
EX = 1
EY = 2
EZ = 16
ITERS = 3
NODES_EL = 512
ELEM_DEV = 32
ELEMS = 32768
NX = 128
NY = 128
NZ = 1024
N_GX = 16
N_GY = 8
N_GZ = 8
DEVICES = 1024


def draw_right_side(key, part):
    full_shape = (COMPS, NODES_EL, ELEMS)
    return jnp.clip(jax.random.normal(key, full_shape, jnp.float32), -6.0, 6.0)


def draw_geometry(key, part):
    key_scale = jax.random.fold_in(key, 11)
    key_link = jax.random.fold_in(key, 12)
    lattice_shape = (3, NX, NY, NZ)
    scales = jnp.exp(jax.random.uniform(key_scale, lattice_shape, jnp.float32, math.log(0.6), math.log(1.6)))
    links = jax.random.uniform(key_link, lattice_shape, jnp.float32, -0.35, 0.35)
    return jnp.stack([scales[0] * scales[0], scales[1] * scales[1], scales[2] * scales[2], links[0] * scales[0] * scales[1], links[1] * scales[0] * scales[2], links[2] * scales[1] * scales[2]])


def plant(drawn, own_key, smallest, largest):
    longest = drawn.shape.index(max(drawn.shape))
    spots = []
    for shift in (0, 1):
        where = [jax.random.randint(jax.random.fold_in(own_key, axis), (), 0, length) for axis, length in enumerate(drawn.shape)]
        where[longest] = (where[longest] + shift) % drawn.shape[longest]
        spots.append(tuple(where))
    return drawn.at[spots[0]].set(smallest).at[spots[1]].set(largest)


def steps_of(key, shape, cuts, low, largest):
    loudness = 1.0
    for axis_at, shards_of in cuts:
        steps = jax.random.uniform(jax.random.fold_in(jax.random.fold_in(key, 6), axis_at), (shards_of,), jnp.float32, low / len(cuts), largest / len(cuts))
        loudness = loudness * jnp.repeat(jnp.exp(steps), shape[axis_at] // shards_of).reshape((-1,) + (1,) * (len(shape) - 1 - axis_at))
    return loudness


def setup_inputs(seed: int = 0) -> dict:
    arg_keys = jax.random.split(jax.random.key(seed), 8)
    return {
        "right_side": draw_right_side(jax.random.fold_in(arg_keys[7], 71), 0),
        "geometry": draw_geometry(jax.random.fold_in(arg_keys[7], 71), 0),
        "viscosity": jnp.clip(jnp.exp(math.log(3.0) - 2.3025851 * jax.random.uniform(arg_keys[2], (NX, NY, NZ), jnp.float32) ** steps_of(arg_keys[2], (NX, NY, NZ), ((0, 16), (1, 8), (2, 8)), -0.2, 0.2)), 0.3, 3.0),
        "eig_low": jnp.clip(jax.random.uniform(arg_keys[3], (1,), jnp.float32, 0.2, 2.0), 0.2, 2.0),
        "eig_high": jnp.clip(jax.random.uniform(arg_keys[4], (1,), jnp.float32, 8.0, 12.0), 8.0, 12.0),
        "element_slot": jax.vmap(lambda own: jax.random.permutation(own, ELEM_DEV))(jax.random.split(arg_keys[5], DEVICES)).reshape((DEVICES, ELEM_DEV)).astype(jnp.int32),
        "dirichlet": plant((jax.random.randint(arg_keys[6], (2, COMPS, NY, NZ), 0, 3) < 1).astype(jnp.int32), jax.random.fold_in(arg_keys[6], 1), 0, 1),
    }


helm_coefficient = 10.0


def legendre_pair(values, degree):
    previous = 0.0 * values + 1.0
    current = values.copy()
    for order in range(2, degree + 1):
        previous, current = current, ((2 * order - 1) * values * current - (order - 1) * previous) / order
    return current, previous


def gll_tables(degree):
    start = np.cos(np.pi * np.arange(degree + 1) / degree)
    nodes_now = start.copy()
    for sweep in range(80):
        top_value, lower_value = legendre_pair(nodes_now, degree)
        nodes_now = nodes_now - (nodes_now * top_value - lower_value) / ((degree + 1) * top_value)
    gll_nodes = nodes_now[::-1].copy()
    gll_nodes[0] = -1.0
    gll_nodes[degree] = 1.0
    legendre_values = legendre_pair(gll_nodes, degree)[0]
    weights = 2.0 / (degree * (degree + 1) * legendre_values ** 2)
    differences = gll_nodes[:, None] - gll_nodes[None, :] + np.eye(degree + 1)
    derivative = legendre_values[:, None] / legendre_values[None, :] / differences
    derivative = derivative * (1.0 - np.eye(degree + 1))
    derivative[0, 0] = -degree * (degree + 1) / 4.0
    derivative[degree, degree] = degree * (degree + 1) / 4.0
    return weights, derivative


def pad_dimension(lattice, dimension):
    widths = [(0, 0)] * lattice.ndim
    widths[dimension] = (1, 1)
    return jnp.pad(lattice, widths)


def fold_rims(extended, dimension, points):
    length = extended.shape[dimension] - 2
    center = lax.slice_in_dim(extended, 1, length + 1, axis=dimension)
    upper_side = lax.slice_in_dim(extended, 2, length + 2, axis=dimension)
    lower_side = lax.slice_in_dim(extended, 0, length, axis=dimension)
    shape_ones = [1] * extended.ndim
    shape_ones[dimension] = length
    position = (jnp.arange(length, dtype=jnp.int32) % points).reshape(tuple(shape_ones))
    upper_flag = (position == points - 1).astype(extended.dtype)
    lower_flag = (position == 0).astype(extended.dtype)
    return center + upper_flag * upper_side + lower_flag * lower_side


def assemble_global(lattice, points):
    for dimension in range(3):
        lattice = fold_rims(pad_dimension(lattice, dimension), dimension, points)
    return lattice


def along(lattice, matrix, dimension, points):
    full_shape = lattice.shape
    split_shape = full_shape[:dimension] + (full_shape[dimension] // points, points) + full_shape[dimension + 1:]
    moved = jnp.moveaxis(lattice.reshape(split_shape), dimension + 1, -1)
    result = jnp.einsum("...i,ai->...a", moved, matrix, precision=lax.Precision.HIGHEST)
    return jnp.moveaxis(result, -1, dimension + 1).reshape(full_shape)


def helmholtz(lattice, geometry, weighted, mass, forward, points):
    slope_first = along(lattice, forward, 0, points)
    slope_second = along(lattice, forward, 1, points)
    slope_third = along(lattice, forward, 2, points)
    flux_first = weighted * (geometry[0] * slope_first + geometry[3] * slope_second + geometry[4] * slope_third)
    flux_second = weighted * (geometry[3] * slope_first + geometry[1] * slope_second + geometry[5] * slope_third)
    flux_third = weighted * (geometry[4] * slope_first + geometry[5] * slope_second + geometry[2] * slope_third)
    backward = forward.T
    return along(flux_first, backward, 0, points) + along(flux_second, backward, 1, points) + along(flux_third, backward, 2, points) + mass * lattice


def reference(right_side, geometry, viscosity, eig_low, eig_high, element_slot, dirichlet):
    points = DEGREE + 1
    weights, derivative = gll_tables(DEGREE)
    forward = jnp.asarray(derivative, jnp.float32)
    squared = forward * forward
    weight_table = jnp.asarray(weights, jnp.float32)
    diagonal_table = jnp.diagonal(forward)
    quadrature = (jnp.tile(weight_table, NX // points)[:, None, None] * jnp.tile(weight_table, NY // points)[None, :, None]) * jnp.tile(weight_table, NZ // points)[None, None, :]
    weighted = quadrature * viscosity
    determinant = (geometry[0] * (geometry[1] * geometry[2] - geometry[5] * geometry[5]) - geometry[3] * (geometry[3] * geometry[2] - geometry[5] * geometry[4]) + geometry[4] * (geometry[3] * geometry[5] - geometry[1] * geometry[4]))
    mass = helm_coefficient * quadrature * determinant
    end_first = jnp.tile(diagonal_table, NX // points)[:, None, None]
    end_second = jnp.tile(diagonal_table, NY // points)[None, :, None]
    end_third = jnp.tile(diagonal_table, NZ // points)[None, None, :]
    cross = 2.0 * weighted * (end_first * end_second * geometry[3] + end_first * end_third * geometry[4] + end_second * end_third * geometry[5])
    diagonal_local = (along(weighted * geometry[0], squared.T, 0, points) + along(weighted * geometry[1], squared.T, 1, points) + along(weighted * geometry[2], squared.T, 2, points)) + cross + mass
    diagonal_sum = assemble_global(diagonal_local, points)

    blocks = right_side.reshape(COMPS, NODES_EL, DEVICES, ELEM_DEV)
    inverse = jnp.argsort(element_slot, axis=1).astype(jnp.int32)
    bricks = jnp.take_along_axis(blocks, jnp.broadcast_to(inverse[None, None], blocks.shape), axis=3)
    bricks = bricks.reshape(COMPS, points, points, points, N_GX, N_GY, N_GZ, EX, EY, EZ)
    rhs_lattice = bricks.transpose(0, 4, 7, 1, 5, 8, 2, 6, 9, 3).reshape(COMPS, NX, NY, NZ)

    midpoint = (eig_high[0] + eig_low[0]) * 0.5
    halfwidth = (eig_high[0] - eig_low[0]) * 0.5
    ratio_start = midpoint / halfwidth
    middle = jnp.zeros((NX - 2, NY, NZ), jnp.float32)
    solutions = []
    for component in range(COMPS):
        indicator = jnp.concatenate([dirichlet[0, component][None].astype(jnp.float32), middle, dirichlet[1, component][None].astype(jnp.float32)], axis=0)
        keep = jnp.where(assemble_global(indicator, points) > 0.5, 0.0, 1.0).astype(jnp.float32)
        residual = keep * assemble_global(rhs_lattice[component], points)
        scaling = keep / diagonal_sum
        damping = 1.0 / ratio_start
        direction = (scaling * residual) / midpoint
        solution = jnp.zeros_like(residual)
        for iteration in range(ITERS):
            solution = solution + direction
            if iteration < ITERS - 1:
                image = assemble_global(helmholtz(direction, geometry, weighted, mass, forward, points), points)
                residual = residual - keep * image
                damping_next = 1.0 / (2.0 * ratio_start - damping)
                direction = (damping_next * damping) * direction + (2.0 * damping_next / halfwidth) * (scaling * residual)
                damping = damping_next
        solutions.append(solution)
    stacked = jnp.stack(solutions)
    back_bricks = stacked.reshape(COMPS, N_GX, EX, points, N_GY, EY, points, N_GZ, EZ, points)
    back_bricks = back_bricks.transpose(0, 3, 6, 9, 1, 4, 7, 2, 5, 8).reshape(COMPS, NODES_EL, DEVICES, ELEM_DEV)
    slotted = jnp.take_along_axis(back_bricks, jnp.broadcast_to(element_slot[None, None], back_bricks.shape), axis=3)
    return slotted.reshape(COMPS, NODES_EL, ELEMS)
```

```python
import functools

import jax
import jax.numpy as jnp
import numpy as np
from jax import lax
from jax.experimental import pallas as pl
from jax.experimental.pallas import tpu as pltpu
from jax.sharding import PartitionSpec as P

DEGREE = 7
HELM = 10.0
N_FIRST = 5
MESH = pl.DeviceIdType.MESH

SIDES = ((-1, 0), (1, 0), (0, -1), (0, 1), (-1, -1), (-1, 1), (1, -1), (1, 1))


def legendre_pair(values, degree):
    previous = 0.0 * values + 1.0
    current = values.copy()
    for order in range(2, degree + 1):
        previous, current = (
            current,
            ((2 * order - 1) * values * current - (order - 1) * previous) / order,
        )
    return (current, previous)


def gll_tables(degree):
    start = np.cos(np.pi * np.arange(degree + 1) / degree)
    nodes_now = start.copy()
    for sweep in range(80):
        top_value, lower_value = legendre_pair(nodes_now, degree)
        nodes_now = nodes_now - (nodes_now * top_value - lower_value) / ((degree + 1) * top_value)
    gll_nodes = nodes_now[::-1].copy()
    gll_nodes[0] = -1.0
    gll_nodes[degree] = 1.0
    legendre_values = legendre_pair(gll_nodes, degree)[0]
    weights = 2.0 / (degree * (degree + 1) * legendre_values**2)
    differences = gll_nodes[:, None] - gll_nodes[None, :] + np.eye(degree + 1)
    derivative = legendre_values[:, None] / legendre_values[None, :] / differences
    derivative = derivative * (1.0 - np.eye(degree + 1))
    derivative[0, 0] = -degree * (degree + 1) / 4.0
    derivative[degree, degree] = degree * (degree + 1) / 4.0
    return (weights, derivative)


WEIGHTS, DERIVATIVE = gll_tables(DEGREE)
DF = DERIVATIVE.astype(np.float32)
WF = WEIGHTS.astype(np.float32)
DS = DF * DF
ENDS = np.diagonal(DF)


def lane_table():
    sub = np.arange(8)
    tiles = []
    for matrix in (DF, DF.T, DS.T):
        for turn in range(8):
            tiles.append(np.repeat(matrix[sub, (sub - turn) % 8][:, None], 128, axis=1))
    lane = np.arange(128) % 8
    tiles.append(WF[:, None] * WF[lane][None, :])
    tiles.append(2.0 * ENDS[:, None] * ENDS[lane][None, :])
    tiles.append(np.repeat(2.0 * ENDS[:, None], 128, axis=1))
    tiles.append(np.repeat(2.0 * ENDS[lane][None, :], 8, axis=0))
    return np.stack(tiles).astype(np.float32)


def lane_matrices():
    import ml_dtypes

    out = []
    for matrix in (DF.T, DF, DS):
        wide = np.kron(np.eye(16, dtype=np.float32), matrix).astype(np.float32)
        high = wide.astype(ml_dtypes.bfloat16)
        low = (wide - high.astype(np.float32)).astype(ml_dtypes.bfloat16)
        half = np.concatenate([high, low], axis=1)
        out.append(np.concatenate([half, half], axis=0))
    return np.stack(out)


def halves(x):
    high = x.astype(jnp.bfloat16)
    low = (x - high.astype(jnp.float32)).astype(jnp.bfloat16)
    return high, low


def slot_matrix(slot):
    row = lax.broadcasted_iota(jnp.int32, (32, 32), 0)
    element = (row & 16) + ((16 - (row & 15)) & 15)
    return jnp.where(jnp.broadcast_to(slot, (32, 32)) == element, 1.0, 0.0).astype(jnp.float32)


def turn_columns(a, b, down):
    sub = lax.broadcasted_iota(jnp.int32, a.shape, 1)
    group = lax.broadcasted_iota(jnp.int32, a.shape, 2) // 8
    for bit in (1, 2, 4):
        here = (group & bit) != 0
        if down:
            ra, rb = pltpu.roll(a, bit, 1), pltpu.roll(b, bit, 1)
            na, nb = jnp.where(sub < bit, rb, ra), jnp.where(sub < bit, ra, rb)
        else:
            ra, rb = pltpu.roll(a, 8 - bit, 1), pltpu.roll(b, 8 - bit, 1)
            na, nb = jnp.where(sub < 8 - bit, ra, rb), jnp.where(sub < 8 - bit, rb, ra)
        a, b = jnp.where(here, na, a), jnp.where(here, nb, b)
    here = (group & 8) != 0
    return jnp.where(here, b, a), jnp.where(here, a, b)


def lane_turn(x, left):
    if not left:
        return pltpu.roll(x, 0, 1, stride=8, stride_axis=0)
    row = lax.broadcasted_iota(jnp.int32, x.shape, 0)
    for bit in (1, 2, 4, 8):
        x = jnp.where((row & bit) != 0, pltpu.roll(x, 128 - 8 * bit, 1), x)
    return x


def along_first(matrix, field):
    planes = [field[2 * i : 2 * i + 2] for i in range(8)]
    out = []
    for a in range(8):
        total = None
        for i in range(8):
            if abs(matrix[a, i]) > 0:
                term = planes[i] * float(matrix[a, i])
                total = term if total is None else total + term
        out.append(total)
    return jnp.concatenate(out, axis=0)


def along_second(tab, base, field):
    total = field * tab[base]
    for turn in range(1, 8):
        total = total + pltpu.roll(field, turn, 1) * tab[base + turn]
    return total


def along_third(matrix, field):
    high, low = halves(field.reshape(128, 128))
    both = jnp.dot(
        jnp.concatenate([high, low], axis=1), matrix, preferred_element_type=jnp.float32
    )
    return (both[:, :128] + both[:, 128:]).reshape(16, 8, 128)


def fold_lanes(field):
    lane = lax.broadcasted_iota(jnp.int32, field.shape, 2)
    upper = (lane % 8 == 7) & (lane < 127)
    lower = (lane % 8 == 0) & (lane > 0)
    return (
        field
        + jnp.where(upper, pltpu.roll(field, 127, 2), 0.0)
        + jnp.where(lower, pltpu.roll(field, 1, 2), 0.0)
    )


def kernel(
    sizes,
    rs_h, geo_h, vis_h, low_s, high_s, slot_h, dir_h, tab_h, mat_h,
    out,
    rs, geo, vis, slot, dirs, tab, mats, gw, mass, inv, scale, zed, way, flux,
    v0, v1, v2, ysend, zsend, yrecv, zrecv, xrecv,
    in_sem, ysem, yrsem, zsem, zrsem, xsem, xrsem,
):
    n_gx, n_gy, n_gz = sizes
    gx, gy, gz = lax.axis_index("gx"), lax.axis_index("gy"), lax.axis_index("gz")

    loads = [
        pltpu.make_async_copy(src, dst, in_sem.at[k])
        for k, (src, dst) in enumerate(
            (
                (rs_h, rs),
                (slot_h, slot),
                (geo_h, geo),
                (vis_h, vis),
                (tab_h, tab),
                (mat_h, mats),
                (dir_h, dirs),
            )
        )
    ]
    for load in loads:
        load.start()

    def inside(step_y, step_z):
        ok = None
        for step, at, size in ((step_y, gy, n_gy), (step_z, gz, n_gz)):
            if step:
                here = (at + step >= 0) & (at + step < size)
                ok = here if ok is None else ok & here
        return ok

    def device(step_y, step_z):
        return {"gx": gx, "gy": gy + step_y, "gz": gz + step_z}

    yrecv[...] = jnp.zeros_like(yrecv)
    zrecv[...] = jnp.zeros_like(zrecv)
    xrecv[...] = jnp.zeros_like(xrecv)

    barrier = pltpu.get_barrier_semaphore()
    count = 0
    for step_y, step_z in SIDES:
        here = inside(step_y, step_z)
        count = count + jnp.where(here, 1, 0)

        @pl.when(here)
        def _():
            pl.semaphore_signal(
                barrier, inc=1, device_id=device(step_y, step_z), device_id_type=MESH
            )

    for step in (-1, 1):
        here = (gx + step >= 0) & (gx + step < n_gx)
        count = count + jnp.where(here, 1, 0)

        @pl.when(here)
        def _():
            pl.semaphore_signal(
                barrier,
                inc=1,
                device_id={"gx": gx + step, "gy": gy, "gz": gz},
                device_id_type=MESH,
            )

    def side_copy(rnd, side, fields):
        step_y, step_z = SIDES[side]
        back = SIDES.index((-step_y, -step_z))
        if side < 2:
            part = (pl.ds(0, fields),)
            return lambda to: pltpu.make_async_remote_copy(
                src_ref=ysend.at[(rnd, side) + part],
                dst_ref=yrecv.at[(rnd, back if to else side) + part],
                send_sem=ysem.at[rnd, side],
                recv_sem=yrsem.at[rnd, back if to else side],
                device_id=device(step_y, step_z),
                device_id_type=MESH,
            )
        part = (pl.ds(0, 2 if fields > 3 else 1),)
        return lambda to: pltpu.make_async_remote_copy(
            src_ref=zsend.at[(rnd,) + part],
            dst_ref=zrecv.at[(rnd, (back if to else side) - 2) + part],
            send_sem=zsem.at[rnd, side - 2],
            recv_sem=zrsem.at[rnd, (back if to else side) - 2],
            device_id=device(step_y, step_z),
            device_id_type=MESH,
        )

    def first_copy(rnd, v, side, fields, to):
        step = (-1, 1)[side]
        plane = (0, 112)[side]
        return pltpu.make_async_remote_copy(
            src_ref=v.at[pl.ds(0, fields), pl.ds(plane, 16)],
            dst_ref=xrecv.at[rnd, (1 - side) if to else side, pl.ds(0, fields)],
            send_sem=xsem.at[rnd, side],
            recv_sem=xrsem.at[rnd, (1 - side) if to else side],
            device_id={"gx": gx + step, "gy": gy, "gz": gz},
            device_id_type=MESH,
        )

    def packed(v, fields):
        lane = lax.broadcasted_iota(jnp.int32, (8, 128), 1) // 2
        groups = [[(f, t) for f in range(3) for t in range(16)]]
        if fields > 3:
            groups.append([(3, t) for t in range(16)] + [(4, t) for t in range(6)])
        for n, group in enumerate(groups):
            parts = [None] * 4
            for q, (f, t) in enumerate(group):
                moved = pltpu.roll(v[f, pl.ds(8 * t, 8), :], 2 * q + 1, 1)
                old = parts[q % 4]
                parts[q % 4] = moved if old is None else jnp.where(lane == q, moved, old)
            for k in range(1, 4):
                parts[0] = jnp.where(lane % 4 == k, parts[k], parts[0])
            yield n, group, parts[0]

    def exchange(rnd, v, fields, x_fields):
        for f in range(fields):
            row7, row8 = v[f, pl.ds(7, 8, stride=16), :], v[f, pl.ds(8, 8, stride=16), :]
            v[f, pl.ds(7, 8, stride=16), :] = row7 + row8
            v[f, pl.ds(8, 8, stride=16), :] = row7 + row8
            ysend[rnd, 0, f] = v[f, pl.ds(0, 8, stride=16), :]
            ysend[rnd, 1, f] = v[f, pl.ds(15, 8, stride=16), :]
        groups = []
        for n, group, tile in packed(v, fields):
            zsend[rnd, n] = tile
            groups.append(group)
        if rnd == 0:
            pl.semaphore_wait(barrier, count)
        for side, (step_y, step_z) in enumerate(SIDES):

            @pl.when(inside(step_y, step_z))
            def _():
                side_copy(rnd, side, fields)(True).start()

        for side, (step_y, step_z) in enumerate(SIDES):

            @pl.when(inside(step_y, step_z))
            def _():
                side_copy(rnd, side, fields)(False).wait_recv()

        lane = lax.broadcasted_iota(jnp.int32, (8, 128), 1)
        sub = lax.broadcasted_iota(jnp.int32, (8, 128), 0)
        odd = lane % 2 == 1
        rim = (lane == 0) | (lane == 127)

        def swapped(minus, plus):
            return jnp.where(odd, pltpu.roll(minus, 1, 1), pltpu.roll(plus, 127, 1))

        for n, group in enumerate(groups):
            near = swapped(zrecv[rnd, 0, n], zrecv[rnd, 1, n])
            below = swapped(zrecv[rnd, 2, n], zrecv[rnd, 3, n])
            above = swapped(zrecv[rnd, 4, n], zrecv[rnd, 5, n])
            below = pltpu.roll(pltpu.roll(below, 1, 0), 126, 1)
            above = pltpu.roll(pltpu.roll(above, 7, 0), 2, 1)
            upper_tile = (lane // 2) % 2 == 1
            near = near + jnp.where((sub == 0) & ~upper_tile, below, 0.0)
            near = near + jnp.where((sub == 7) & upper_tile, above, 0.0)
            order = sorted(range(len(group)), key=lambda q: group[q][1] not in (0, 1, 14, 15))
            for q in order:
                f, t = group[q]
                moved = pltpu.roll(near, (128 - (2 * q + 1)) % 128, 1)
                v[f, pl.ds(8 * t, 8), :] = v[f, pl.ds(8 * t, 8), :] + jnp.where(rim, moved, 0.0)
        for f in range(fields):
            for side, row in ((0, 0), (1, 15)):
                rows = pl.ds(row, 8, stride=16)
                v[f, rows, :] = v[f, rows, :] + yrecv[rnd, side, f]
        for side, step in enumerate((-1, 1)):

            @pl.when((gx + step >= 0) & (gx + step < n_gx))
            def _():
                first_copy(rnd, v, side, x_fields, True).start()

    def arrive(rnd, v, x_fields):
        for side, step in enumerate((-1, 1)):

            @pl.when((gx + step >= 0) & (gx + step < n_gx))
            def _():
                first_copy(rnd, v, side, x_fields, False).wait_recv()

    def field_of(v, f):
        return v[f].reshape(16, 8, 128)

    def whole(rnd, v, f):
        own = field_of(v, f)
        return jnp.concatenate(
            [
                own[:2] + xrecv[rnd, 0, f].reshape(2, 8, 128),
                own[2:14],
                own[14:] + xrecv[rnd, 1, f].reshape(2, 8, 128),
            ],
            axis=0,
        )

    loads[0].wait()
    loads[1].wait()
    one_hot = slot_matrix(slot[...]).astype(jnp.bfloat16)
    pair = jnp.concatenate([one_hot, one_hot], axis=1)
    blocks = []
    for c in range(3):
        high, low = halves(rs[c])
        placed = jnp.dot(
            pair, jnp.concatenate([high, low], axis=0), preferred_element_type=jnp.float32
        )
        for ip in range(4):
            blocks.append(placed[:, 128 * ip : 128 * ip + 128])
    rows = lane_turn(jnp.concatenate(blocks, axis=0), True).reshape(24, 2, 8, 128)
    a, b = turn_columns(rows[:, 0], rows[:, 1], True)
    rows = jnp.stack([a, b], axis=1).reshape(384, 128)
    rows = lane_turn(rows, True).reshape(3, 4, 2, 2, 8, 128)
    for c in range(3):
        field = jnp.stack([rows[c, :, 0], rows[c, :, 1]], axis=2).reshape(16, 8, 128)
        v0[c] = fold_lanes(field).reshape(128, 128)

    for load in loads[2:]:
        load.wait()

    quad = tab[24]
    for x in range(8):
        at = pl.ds(2 * x, 2)
        xx, yy, zz, xy, xz, yz = (geo[k, at] for k in range(6))
        quad_x = quad * float(WF[x])
        weighted = quad_x * vis[at]
        det = (
            xx * (yy * zz - yz * yz) - xy * (xy * zz - yz * xz) + xz * (xy * yz - yy * xz)
        )
        mass_x = (HELM * quad_x) * det
        mass[at] = mass_x
        for k, g in enumerate((xx, yy, zz, xy, xz, yz)):
            gw[k, at] = weighted * g
        cross = (weighted * yz) * tab[25] + mass_x
        if x in (0, 7):
            end = float(ENDS[x])
            cross = cross + (weighted * xy) * (tab[26] * end) + (weighted * xz) * (tab[27] * end)
        zed[0, at] = cross
    local = (
        along_first(DS.T, gw[0])
        + along_second(tab, 16, gw[1])
        + along_third(mats[2], gw[2])
        + zed[0]
    )
    v0[3] = fold_lanes(local).reshape(128, 128)

    low_end = jnp.where(gx == 0, 1.0, 0.0)
    high_end = jnp.where(gx == n_gx - 1, 1.0, 0.0)
    marks = dirs[0].astype(jnp.float32) * low_end + dirs[1].astype(jnp.float32) * high_end
    v0[4] = jnp.zeros((128, 128), jnp.float32)
    v0[4, :48] = fold_lanes(marks.reshape(6, 8, 128)).reshape(48, 128)

    exchange(0, v0, N_FIRST, 4)

    low = jnp.full((8, 128), low_s[0], jnp.float32)
    high = jnp.full((8, 128), high_s[0], jnp.float32)
    middle, half = (high + low) * 0.5, (high - low) * 0.5
    ratio = middle / half
    damping = 1.0 / ratio
    factors = []
    for _ in range(2):
        following = 1.0 / (2.0 * ratio - damping)
        factors.append((following * damping, 2.0 * following / half))
        damping = following

    arrive(0, v0, 4)
    inverse = 1.0 / whole(0, v0, 3)
    inv[...] = inverse
    for c in range(3):
        flags = v0[4, pl.ds(16 * c, 16), :].reshape(2, 8, 128)
        free = jnp.where(flags > 0.5, 0.0, 1.0)
        keep_low = free * low_end + (1.0 - low_end)
        keep_high = free * high_end + (1.0 - high_end)
        scale[c, 0] = inverse[:2] * keep_low
        scale[c, 1] = inverse[14:] * keep_high

    def scaled(c, field):
        return jnp.concatenate(
            [scale[c, 0] * field[:2], inv[pl.ds(2, 12)] * field[2:14], scale[c, 1] * field[14:]],
            axis=0,
        )

    for c in range(3):
        start = scaled(c, whole(0, v0, c))
        zed[c] = start
        way[c] = start / middle
        out[c] = way[c].reshape(128, 128)

    for rnd, v in ((1, v1), (2, v2)):
        for c in range(3):
            field = way[c]
            slope1 = along_first(DF, field)
            slope2 = along_second(tab, 0, field)
            slope3 = along_third(mats[0], field)
            flux[0] = gw[0] * slope1 + gw[3] * slope2 + gw[4] * slope3
            flux[1] = gw[3] * slope1 + gw[1] * slope2 + gw[5] * slope3
            flux[2] = gw[4] * slope1 + gw[5] * slope2 + gw[2] * slope3
            image = (
                along_first(DF.T, flux[0])
                + along_second(tab, 8, flux[1])
                + along_third(mats[1], flux[2])
                + mass[...] * field
            )
            v[c] = fold_lanes(image).reshape(128, 128)
        exchange(rnd, v, 3, 3)
        arrive(rnd, v, 3)
        keep_by, add_by = factors[rnd - 1]
        for c in range(3):
            rest = zed[c] - scaled(c, whole(rnd, v, c))
            zed[c] = rest
            step = keep_by * way[c] + add_by * rest
            way[c] = step
            out[c] = out[c] + step.reshape(128, 128)

    for rnd, v, fields, x_fields in ((0, v0, N_FIRST, 4), (1, v1, 3, 3), (2, v2, 3, 3)):
        for side, (step_y, step_z) in enumerate(SIDES):

            @pl.when(inside(step_y, step_z))
            def _():
                side_copy(rnd, side, fields)(True).wait_send()

        for side, step in enumerate((-1, 1)):

            @pl.when((gx + step >= 0) & (gx + step < n_gx))
            def _():
                first_copy(rnd, v, side, x_fields, True).wait_send()


def to_slots(field, slot, out):
    rows = field[...].reshape(3, 4, 2, 2, 8, 128)
    rows = jnp.stack([rows[:, :, 0], rows[:, :, 1]], axis=3).reshape(384, 128)
    rows = lane_turn(rows, False).reshape(24, 2, 8, 128)
    a, b = turn_columns(rows[:, 0], rows[:, 1], False)
    rows = lane_turn(jnp.stack([a, b], axis=1).reshape(384, 128), False).reshape(3, 4, 32, 128)
    one_hot = slot_matrix(slot[...]).T.astype(jnp.bfloat16)
    pair = jnp.concatenate([one_hot, one_hot], axis=1)
    for c in range(3):
        wide = jnp.concatenate([rows[c, ip] for ip in range(4)], axis=1)
        high, low = halves(wide)
        out[c] = jnp.dot(
            pair, jnp.concatenate([high, low], axis=0), preferred_element_type=jnp.float32
        )


def shards(sizes, right_side, geometry, viscosity, eig_low, eig_high, element_slot, dirichlet):
    f32 = jnp.float32
    anywhere = pl.BlockSpec(memory_space=pl.ANY)
    scalar = pl.BlockSpec(memory_space=pltpu.SMEM)
    vmem = pl.BlockSpec(memory_space=pltpu.VMEM)
    field = pl.pallas_call(
        functools.partial(kernel, sizes),
        out_shape=jax.ShapeDtypeStruct((3, 128, 128), f32),
        in_specs=[anywhere] * 3 + [scalar] * 2 + [anywhere] * 4,
        out_specs=vmem,
        scratch_shapes=[
            pltpu.VMEM((3, 32, 512), f32),
            pltpu.VMEM((6, 16, 8, 128), f32),
            pltpu.VMEM((16, 8, 128), f32),
            pltpu.VMEM((1, 32), jnp.int32),
            pltpu.VMEM((2, 3, 16, 128), jnp.int32),
            pltpu.VMEM((28, 8, 128), f32),
            pltpu.VMEM((3, 256, 256), jnp.bfloat16),
            pltpu.VMEM((6, 16, 8, 128), f32),
            pltpu.VMEM((16, 8, 128), f32),
            pltpu.VMEM((16, 8, 128), f32),
            pltpu.VMEM((3, 2, 2, 8, 128), f32),
            pltpu.VMEM((3, 16, 8, 128), f32),
            pltpu.VMEM((3, 16, 8, 128), f32),
            pltpu.VMEM((3, 16, 8, 128), f32),
            pltpu.VMEM((5, 128, 128), f32),
            pltpu.VMEM((3, 128, 128), f32),
            pltpu.VMEM((3, 128, 128), f32),
            pltpu.VMEM((3, 2, 5, 8, 128), f32),
            pltpu.VMEM((3, 2, 8, 128), f32),
            pltpu.VMEM((3, 2, 5, 8, 128), f32),
            pltpu.VMEM((3, 6, 2, 8, 128), f32),
            pltpu.VMEM((3, 2, 4, 16, 128), f32),
            pltpu.SemaphoreType.DMA((7,)),
            pltpu.SemaphoreType.DMA((3, 2)),
            pltpu.SemaphoreType.DMA((3, 2)),
            pltpu.SemaphoreType.DMA((3, 6)),
            pltpu.SemaphoreType.DMA((3, 6)),
            pltpu.SemaphoreType.DMA((3, 2)),
            pltpu.SemaphoreType.DMA((3, 2)),
        ],
        compiler_params=pltpu.CompilerParams(collective_id=0, has_side_effects=True),
        name="solve",
    )(
        jnp.swapaxes(right_side, 1, 2),
        geometry.reshape(6, 16, 8, 128),
        viscosity.reshape(16, 8, 128),
        eig_low,
        eig_high,
        element_slot,
        dirichlet,
        jnp.asarray(lane_table()),
        jnp.asarray(lane_matrices()),
    )
    slots = pl.pallas_call(
        to_slots,
        out_shape=jax.ShapeDtypeStruct((3, 32, 512), f32),
        in_specs=[vmem, vmem],
        out_specs=vmem,
        name="to_slots",
    )(field.reshape(3, 16, 8, 128), element_slot)
    return jnp.swapaxes(slots, 1, 2)


def solution(mesh):
    sizes = tuple(mesh.shape[axis] for axis in ("gx", "gy", "gz"))
    return jax.shard_map(
        functools.partial(shards, sizes),
        mesh=mesh,
        in_specs=(
            P(None, None, ("gx", "gy", "gz")),
            P(None, "gx", "gy", "gz"),
            P("gx", "gy", "gz"),
            P(),
            P(),
            P(("gx", "gy", "gz"), None),
            P(None, None, "gy", "gz"),
        ),
        out_specs=P(None, None, ("gx", "gy", "gz")),
        check_vma=False,
    )
```

```python
import functools

import jax
import jax.numpy as jnp
import numpy as np
from jax import lax
from jax.experimental import pallas as pl
from jax.experimental.pallas import tpu as pltpu
from jax.sharding import PartitionSpec as P

DEGREE = 7
HELM = 10.0
N_FIRST = 5
MESH = pl.DeviceIdType.MESH

SIDES = ((-1, 0), (1, 0), (0, -1), (0, 1), (-1, -1), (-1, 1), (1, -1), (1, 1))


def legendre_pair(values, degree):
    previous = 0.0 * values + 1.0
    current = values.copy()
    for order in range(2, degree + 1):
        previous, current = (
            current,
            ((2 * order - 1) * values * current - (order - 1) * previous) / order,
        )
    return (current, previous)


def gll_tables(degree):
    start = np.cos(np.pi * np.arange(degree + 1) / degree)
    nodes_now = start.copy()
    for sweep in range(80):
        top_value, lower_value = legendre_pair(nodes_now, degree)
        nodes_now = nodes_now - (nodes_now * top_value - lower_value) / ((degree + 1) * top_value)
    gll_nodes = nodes_now[::-1].copy()
    gll_nodes[0] = -1.0
    gll_nodes[degree] = 1.0
    legendre_values = legendre_pair(gll_nodes, degree)[0]
    weights = 2.0 / (degree * (degree + 1) * legendre_values**2)
    differences = gll_nodes[:, None] - gll_nodes[None, :] + np.eye(degree + 1)
    derivative = legendre_values[:, None] / legendre_values[None, :] / differences
    derivative = derivative * (1.0 - np.eye(degree + 1))
    derivative[0, 0] = -degree * (degree + 1) / 4.0
    derivative[degree, degree] = degree * (degree + 1) / 4.0
    return (weights, derivative)


WEIGHTS, DERIVATIVE = gll_tables(DEGREE)
DF = DERIVATIVE.astype(np.float32)
WF = WEIGHTS.astype(np.float32)
DS = DF * DF
ENDS = np.diagonal(DF)


def lane_table():
    sub = np.arange(8)
    tiles = []
    for matrix in (DF, DF.T, DS.T):
        for turn in range(8):
            tiles.append(np.repeat(matrix[sub, (sub - turn) % 8][:, None], 128, axis=1))
    lane = np.arange(128) % 8
    tiles.append(WF[:, None] * WF[lane][None, :])
    tiles.append(2.0 * ENDS[:, None] * ENDS[lane][None, :])
    tiles.append(np.repeat(2.0 * ENDS[:, None], 128, axis=1))
    tiles.append(np.repeat(2.0 * ENDS[lane][None, :], 8, axis=0))
    return np.stack(tiles).astype(np.float32)


def lane_matrices():
    import ml_dtypes

    out = []
    for matrix in (DF.T, DF, DS):
        wide = np.kron(np.eye(16, dtype=np.float32), matrix).astype(np.float32)
        high = wide.astype(ml_dtypes.bfloat16)
        low = (wide - high.astype(np.float32)).astype(ml_dtypes.bfloat16)
        half = np.concatenate([high, low], axis=1)
        out.append(np.concatenate([half, half], axis=0))
    return np.stack(out)


def halves(x):
    high = x.astype(jnp.bfloat16)
    low = (x - high.astype(jnp.float32)).astype(jnp.bfloat16)
    return high, low


def slot_matrix(slot):
    row = lax.broadcasted_iota(jnp.int32, (32, 32), 0)
    element = (row & 16) + ((16 - (row & 15)) & 15)
    return jnp.where(jnp.broadcast_to(slot, (32, 32)) == element, 1.0, 0.0).astype(jnp.float32)


def turn_columns(a, b, down):
    sub = lax.broadcasted_iota(jnp.int32, (8, 128), 0)
    group = lax.broadcasted_iota(jnp.int32, (8, 128), 1) // 8
    start = (sub - group if down else sub + group) & 15
    straight = start < 8
    low, high = [], []
    for n in range(a.shape[0]):
        ta = jnp.take_along_axis(a[n], start & 7, axis=0, mode="promise_in_bounds")
        tb = jnp.take_along_axis(b[n], start & 7, axis=0, mode="promise_in_bounds")
        low.append(jnp.where(straight, ta, tb))
        high.append(jnp.where(straight, tb, ta))
    return jnp.stack(low), jnp.stack(high)


def lane_turn(x, left):
    if not left:
        return pltpu.roll(x, 0, 1, stride=8, stride_axis=0)
    row = lax.broadcasted_iota(jnp.int32, x.shape, 0)
    lane = lax.broadcasted_iota(jnp.int32, x.shape, 1)
    source = (lane + 8 * (row & 15)) & 127
    return jnp.take_along_axis(x, source, axis=1, mode="promise_in_bounds")


def along_first(matrix, planes, outs=range(8)):
    out = []
    for a in outs:
        total = None
        for i, plane in planes.items():
            if abs(matrix[a, i]) > 0:
                term = plane * float(matrix[a, i])
                total = term if total is None else total + term
        out.append(total)
    return jnp.concatenate(out, axis=0)


def planes_of(field, first=0):
    return {first + i: field[2 * i : 2 * i + 2] for i in range(field.shape[0] // 2)}


def along_second(tab, base, field):
    total = field * tab[base]
    for turn in range(1, 8):
        total = total + pltpu.roll(field, turn, 1) * tab[base + turn]
    return total


def along_third(matrix, field):
    high, low = halves(field.reshape(-1, 128))
    both = jnp.dot(
        jnp.concatenate([high, low], axis=1), matrix, preferred_element_type=jnp.float32
    )
    return (both[:, :128] + both[:, 128:]).reshape(field.shape)


def fold_lanes(field):
    lane = lax.broadcasted_iota(jnp.int32, field.shape, 2)
    upper = (lane % 8 == 7) & (lane < 127)
    lower = (lane % 8 == 0) & (lane > 0)
    return (
        field
        + jnp.where(upper, pltpu.roll(field, 127, 2), 0.0)
        + jnp.where(lower, pltpu.roll(field, 1, 2), 0.0)
    )


def kernel(
    sizes,
    rs_h, geo_h, vis_h, low_s, high_s, slot_h, dir_h, tab_h, mat_h,
    out, place,
    rs, geo, vis, slot, dirs, tab, mats, gw, mass, inv, scale, zed, way, flux, edge, total,
    v0, v1, v2, ysend, zsend, yrecv, zrecv, xrecv,
    in_sem, ysem, yrsem, zsem, zrsem, xsem, xrsem,
):
    n_gx, n_gy, n_gz = sizes
    gx, gy, gz = lax.axis_index("gx"), lax.axis_index("gy"), lax.axis_index("gz")

    loads = [
        pltpu.make_async_copy(src, dst, in_sem.at[k])
        for k, (src, dst) in enumerate(
            (
                (rs_h, rs),
                (slot_h, slot),
                (geo_h, geo),
                (vis_h, vis),
                (tab_h, tab),
                (mat_h, mats),
                (dir_h, dirs),
            )
        )
    ]
    for load in loads:
        load.start()

    def inside(step_y, step_z):
        ok = None
        for step, at, size in ((step_y, gy, n_gy), (step_z, gz, n_gz)):
            if step:
                here = (at + step >= 0) & (at + step < size)
                ok = here if ok is None else ok & here
        return ok

    def device(step_y, step_z):
        return {"gx": gx, "gy": gy + step_y, "gz": gz + step_z}

    yrecv[...] = jnp.zeros_like(yrecv)
    zrecv[...] = jnp.zeros_like(zrecv)
    xrecv[...] = jnp.zeros_like(xrecv)

    barrier = pltpu.get_barrier_semaphore()
    count = 0
    for step_y, step_z in SIDES:
        here = inside(step_y, step_z)
        count = count + jnp.where(here, 1, 0)

        @pl.when(here)
        def _():
            pl.semaphore_signal(
                barrier, inc=1, device_id=device(step_y, step_z), device_id_type=MESH
            )

    for step in (-1, 1):
        here = (gx + step >= 0) & (gx + step < n_gx)
        count = count + jnp.where(here, 1, 0)

        @pl.when(here)
        def _():
            pl.semaphore_signal(
                barrier,
                inc=1,
                device_id={"gx": gx + step, "gy": gy, "gz": gz},
                device_id_type=MESH,
            )

    def side_copy(rnd, side, fields):
        step_y, step_z = SIDES[side]
        back = SIDES.index((-step_y, -step_z))
        if side < 2:
            part = (pl.ds(0, fields),)
            return lambda to: pltpu.make_async_remote_copy(
                src_ref=ysend.at[(rnd, side) + part],
                dst_ref=yrecv.at[(rnd, back if to else side) + part],
                send_sem=ysem.at[rnd, side],
                recv_sem=yrsem.at[rnd, back if to else side],
                device_id=device(step_y, step_z),
                device_id_type=MESH,
            )
        part = (pl.ds(0, 2 if fields > 3 else 1),)
        return lambda to: pltpu.make_async_remote_copy(
            src_ref=zsend.at[(rnd,) + part],
            dst_ref=zrecv.at[(rnd, (back if to else side) - 2) + part],
            send_sem=zsem.at[rnd, side - 2],
            recv_sem=zrsem.at[rnd, (back if to else side) - 2],
            device_id=device(step_y, step_z),
            device_id_type=MESH,
        )

    def first_copy(rnd, v, side, fields, to):
        step = (-1, 1)[side]
        plane = (0, 112)[side]
        return pltpu.make_async_remote_copy(
            src_ref=v.at[pl.ds(0, fields), pl.ds(plane, 16)],
            dst_ref=xrecv.at[rnd, (1 - side) if to else side, pl.ds(0, fields)],
            send_sem=xsem.at[rnd, side],
            recv_sem=xrsem.at[rnd, (1 - side) if to else side],
            device_id={"gx": gx + step, "gy": gy, "gz": gz},
            device_id_type=MESH,
        )

    def packed(v, fields):
        lane = lax.broadcasted_iota(jnp.int32, (8, 128), 1) // 2
        groups = [[(f, t) for f in range(3) for t in range(16)]]
        if fields > 3:
            groups.append([(3, t) for t in range(16)] + [(4, t) for t in range(6)])
        for n, group in enumerate(groups):
            parts = [None] * 4
            for q, (f, t) in enumerate(group):
                moved = pltpu.roll(v[f, pl.ds(8 * t, 8), :], 2 * q + 1, 1)
                old = parts[q % 4]
                parts[q % 4] = moved if old is None else jnp.where(lane == q, moved, old)
            for k in range(1, 4):
                parts[0] = jnp.where(lane % 4 == k, parts[k], parts[0])
            yield n, group, parts[0]

    def exchange(rnd, v, fields, x_fields):
        for f in range(fields):
            row7, row8 = v[f, pl.ds(7, 8, stride=16), :], v[f, pl.ds(8, 8, stride=16), :]
            v[f, pl.ds(7, 8, stride=16), :] = row7 + row8
            v[f, pl.ds(8, 8, stride=16), :] = row7 + row8
            ysend[rnd, 0, f] = v[f, pl.ds(0, 8, stride=16), :]
            ysend[rnd, 1, f] = v[f, pl.ds(15, 8, stride=16), :]
        if rnd == 0:
            pl.semaphore_wait(barrier, count)
        for side in (0, 1):

            @pl.when(inside(*SIDES[side]))
            def _():
                side_copy(rnd, side, fields)(True).start()

        groups = []
        for n, group, tile in packed(v, fields):
            zsend[rnd, n] = tile
            groups.append(group)
        for side in (4, 5, 6, 7, 2, 3):

            @pl.when(inside(*SIDES[side]))
            def _():
                side_copy(rnd, side, fields)(True).start()

        for side, (step_y, step_z) in enumerate(SIDES):

            @pl.when(inside(step_y, step_z))
            def _():
                side_copy(rnd, side, fields)(False).wait_recv()

        lane = lax.broadcasted_iota(jnp.int32, (8, 128), 1)
        sub = lax.broadcasted_iota(jnp.int32, (8, 128), 0)
        odd = lane % 2 == 1
        rim = (lane == 0) | (lane == 127)

        def swapped(minus, plus):
            return jnp.where(odd, pltpu.roll(minus, 1, 1), pltpu.roll(plus, 127, 1))

        for f in range(fields):
            for side, row in ((0, 0), (1, 15)):
                rows = pl.ds(row, 8, stride=16)
                v[f, rows, :] = v[f, rows, :] + yrecv[rnd, side, f]
        nears = []
        for n, group in enumerate(groups):
            near = swapped(zrecv[rnd, 0, n], zrecv[rnd, 1, n])
            below = swapped(zrecv[rnd, 2, n], zrecv[rnd, 3, n])
            above = swapped(zrecv[rnd, 4, n], zrecv[rnd, 5, n])
            below = pltpu.roll(pltpu.roll(below, 1, 0), 126, 1)
            above = pltpu.roll(pltpu.roll(above, 7, 0), 2, 1)
            upper_tile = (lane // 2) % 2 == 1
            near = near + jnp.where((sub == 0) & ~upper_tile, below, 0.0)
            nears.append(near + jnp.where((sub == 7) & upper_tile, above, 0.0))

        def unpack(wanted):
            for near, group in zip(nears, groups):
                for q, (f, t) in enumerate(group):
                    if (t in (0, 1, 14, 15) and f < 4) == wanted:
                        moved = pltpu.roll(near, (128 - (2 * q + 1)) % 128, 1)
                        tile = pl.ds(8 * t, 8)
                        v[f, tile, :] = v[f, tile, :] + jnp.where(rim, moved, 0.0)

        unpack(True)
        for side, step in enumerate((-1, 1)):

            @pl.when((gx + step >= 0) & (gx + step < n_gx))
            def _():
                first_copy(rnd, v, side, x_fields, True).start()

        unpack(False)

    def arrive(rnd, v, x_fields):
        for side, step in enumerate((-1, 1)):

            @pl.when((gx + step >= 0) & (gx + step < n_gx))
            def _():
                first_copy(rnd, v, side, x_fields, False).wait_recv()

    inner = pl.ds(2, 12)

    def middle_of(v, f):
        return v[f, pl.ds(16, 96), :].reshape(12, 8, 128)

    def rims_of(rnd, v, f):
        first = v[f, pl.ds(0, 16), :] + xrecv[rnd, 0, f]
        last = v[f, pl.ds(112, 16), :] + xrecv[rnd, 1, f]
        return jnp.concatenate([first.reshape(2, 8, 128), last.reshape(2, 8, 128)], axis=0)

    def put_rims(ref, c, value):
        ref[c, pl.ds(0, 2)] = value[:2]
        ref[c, pl.ds(14, 2)] = value[2:]

    def get_rims(ref, c):
        return jnp.concatenate([ref[c, pl.ds(0, 2)], ref[c, pl.ds(14, 2)]], axis=0)

    def fluxes(c, where, slopes, base=None):
        s1, s2, s3 = slopes
        for k, (a, b, d) in enumerate(((0, 3, 4), (3, 1, 5), (4, 5, 2))):
            flux[c, k, where] = gw[a, where] * s1 + gw[b, where] * s2 + gw[d, where] * s3

    def ahead(c):
        field = way[c, inner]
        planes = planes_of(field, 1)
        edge[c] = along_first(DF, planes, (0, 7))
        fluxes(
            c,
            inner,
            (
                along_first(DF, planes, range(1, 7)),
                along_second(tab, 0, field),
                along_third(mats[0], field),
            ),
        )

    def image_of(c):
        rims = get_rims(way, c)
        ends = {0: rims[:2], 7: rims[2:]}
        s1 = edge[c] + along_first(DF, ends, (0, 7))
        s2 = along_second(tab, 0, rims)
        s3 = along_third(mats[0], rims)
        for n, where in enumerate((pl.ds(0, 2), pl.ds(14, 2))):
            part = slice(2 * n, 2 * n + 2)
            fluxes(c, where, (s1[part], s2[part], s3[part]))
        more = along_first(DF, ends, range(1, 7))
        for k, a in enumerate((0, 3, 4)):
            flux[c, k, inner] = flux[c, k, inner] + gw[a, inner] * more
        return (
            along_first(DF.T, planes_of(flux[c, 0]))
            + along_second(tab, 8, flux[c, 1])
            + along_third(mats[1], flux[c, 2])
            + mass[...] * way[c]
        )

    loads[0].wait()
    loads[1].wait()
    one_hot = slot_matrix(slot[...])
    place[...] = one_hot.T
    one_hot = one_hot.astype(jnp.bfloat16)
    pair = jnp.concatenate([one_hot, one_hot], axis=1)
    blocks = []
    for c in range(3):
        high, low = halves(rs[c])
        placed = jnp.dot(
            pair, jnp.concatenate([high, low], axis=0), preferred_element_type=jnp.float32
        )
        for ip in range(4):
            blocks.append(placed[:, 128 * ip : 128 * ip + 128])
    rows = lane_turn(jnp.concatenate(blocks, axis=0), True).reshape(24, 2, 8, 128)
    a, b = turn_columns(rows[:, 0], rows[:, 1], True)
    rows = jnp.stack([a, b], axis=1).reshape(384, 128)
    rows = lane_turn(rows, True).reshape(3, 4, 2, 2, 8, 128)
    for c in range(3):
        field = jnp.stack([rows[c, :, 0], rows[c, :, 1]], axis=2).reshape(16, 8, 128)
        v0[c] = fold_lanes(field).reshape(128, 128)

    for load in loads[2:]:
        load.wait()

    quad = tab[24]
    for x in range(8):
        at = pl.ds(2 * x, 2)
        xx, yy, zz, xy, xz, yz = (geo[k, at] for k in range(6))
        quad_x = quad * float(WF[x])
        weighted = quad_x * vis[at]
        det = (
            xx * (yy * zz - yz * yz) - xy * (xy * zz - yz * xz) + xz * (xy * yz - yy * xz)
        )
        mass_x = (HELM * quad_x) * det
        mass[at] = mass_x
        for k, g in enumerate((xx, yy, zz, xy, xz, yz)):
            gw[k, at] = weighted * g
        cross = (weighted * yz) * tab[25] + mass_x
        if x in (0, 7):
            end = float(ENDS[x])
            cross = cross + (weighted * xy) * (tab[26] * end) + (weighted * xz) * (tab[27] * end)
        zed[0, at] = cross
    local = (
        along_first(DS.T, planes_of(gw[0]))
        + along_second(tab, 16, gw[1])
        + along_third(mats[2], gw[2])
        + zed[0]
    )
    v0[3] = fold_lanes(local).reshape(128, 128)

    low_end = jnp.where(gx == 0, 1.0, 0.0)
    high_end = jnp.where(gx == n_gx - 1, 1.0, 0.0)
    marks = dirs[0].astype(jnp.float32) * low_end + dirs[1].astype(jnp.float32) * high_end
    v0[4] = jnp.zeros((128, 128), jnp.float32)
    v0[4, :48] = fold_lanes(marks.reshape(6, 8, 128)).reshape(48, 128)

    exchange(0, v0, N_FIRST, 4)

    low = jnp.full((8, 128), low_s[0], jnp.float32)
    high = jnp.full((8, 128), high_s[0], jnp.float32)
    middle, half = (high + low) * 0.5, (high - low) * 0.5
    ratio = middle / half
    damping = 1.0 / ratio
    factors = []
    for _ in range(2):
        following = 1.0 / (2.0 * ratio - damping)
        factors.append((following * damping, 2.0 * following / half))
        damping = following

    inverse = 1.0 / middle_of(v0, 3)
    inv[inner] = inverse
    for c in range(3):
        start = inverse * middle_of(v0, c)
        zed[c, inner] = start
        way[c, inner] = start / middle
        out[c, pl.ds(16, 96), :] = way[c, inner].reshape(96, 128)
    for c in range(3):
        ahead(c)
    arrive(0, v0, 4)
    inverse = 1.0 / rims_of(0, v0, 3)
    for c in range(3):
        flags = v0[4, pl.ds(16 * c, 16), :].reshape(2, 8, 128)
        free = jnp.where(flags > 0.5, 0.0, 1.0)
        keep_low = free * low_end + (1.0 - low_end)
        keep_high = free * high_end + (1.0 - high_end)
        scale[c] = inverse * jnp.concatenate([keep_low, keep_high], axis=0)
        start = scale[c] * rims_of(0, v0, c)
        put_rims(zed, c, start)
        put_rims(way, c, start / middle)

    for rnd, v in ((1, v1), (2, v2)):
        for c in range(3):
            v[c] = fold_lanes(image_of(c)).reshape(128, 128)
        exchange(rnd, v, 3, 3)
        keep_by, add_by = factors[rnd - 1]
        for c in range(3):
            rest = zed[c, inner] - inv[inner] * middle_of(v, c)
            step = keep_by * way[c, inner] + add_by * rest
            out[c, pl.ds(16, 96), :] = out[c, pl.ds(16, 96), :] + step.reshape(96, 128)
            if rnd == 1:
                zed[c, inner] = rest
                way[c, inner] = step
        for c in range(3):
            if rnd == 1:
                ahead(c)
                total[c] = get_rims(way, c)
        arrive(rnd, v, 3)
        for c in range(3):
            rest = get_rims(zed, c) - scale[c] * rims_of(rnd, v, c)
            step = keep_by * get_rims(way, c) + add_by * rest
            if rnd == 1:
                put_rims(zed, c, rest)
                put_rims(way, c, step)
            total[c] = total[c] + step
            if rnd == 2:
                whole = total[c].reshape(32, 128)
                out[c, pl.ds(0, 16), :] = whole[:16]
                out[c, pl.ds(112, 16), :] = whole[16:]

    for rnd, v, fields, x_fields in ((0, v0, N_FIRST, 4), (1, v1, 3, 3), (2, v2, 3, 3)):
        for side, (step_y, step_z) in enumerate(SIDES):

            @pl.when(inside(step_y, step_z))
            def _():
                side_copy(rnd, side, fields)(True).wait_send()

        for side, step in enumerate((-1, 1)):

            @pl.when((gx + step >= 0) & (gx + step < n_gx))
            def _():
                first_copy(rnd, v, side, x_fields, True).wait_send()


def to_slots(field, place, out):
    rows = field[...].reshape(3, 4, 2, 2, 8, 128)
    rows = jnp.stack([rows[:, :, 0], rows[:, :, 1]], axis=3).reshape(384, 128)
    rows = lane_turn(rows, False).reshape(24, 2, 8, 128)
    a, b = turn_columns(rows[:, 0], rows[:, 1], False)
    rows = lane_turn(jnp.stack([a, b], axis=1).reshape(384, 128), False).reshape(3, 4, 32, 128)
    one_hot = place[...].astype(jnp.bfloat16)
    pair = jnp.concatenate([one_hot, one_hot], axis=1)
    for c in range(3):
        wide = jnp.concatenate([rows[c, ip] for ip in range(4)], axis=1)
        high, low = halves(wide)
        out[c] = jnp.dot(
            pair, jnp.concatenate([high, low], axis=0), preferred_element_type=jnp.float32
        )


def shards(sizes, right_side, geometry, viscosity, eig_low, eig_high, element_slot, dirichlet):
    f32 = jnp.float32
    anywhere = pl.BlockSpec(memory_space=pl.ANY)
    scalar = pl.BlockSpec(memory_space=pltpu.SMEM)
    vmem = pl.BlockSpec(memory_space=pltpu.VMEM)
    field, place = pl.pallas_call(
        functools.partial(kernel, sizes),
        out_shape=(pltpu.VMEM((3, 128, 128), f32), pltpu.VMEM((32, 32), f32)),
        in_specs=[anywhere] * 3 + [scalar] * 2 + [anywhere] * 4,
        out_specs=(vmem, vmem),
        scratch_shapes=[
            pltpu.VMEM((3, 32, 512), f32),
            pltpu.VMEM((6, 16, 8, 128), f32),
            pltpu.VMEM((16, 8, 128), f32),
            pltpu.VMEM((1, 32), jnp.int32),
            pltpu.VMEM((2, 3, 16, 128), jnp.int32),
            pltpu.VMEM((28, 8, 128), f32),
            pltpu.VMEM((3, 256, 256), jnp.bfloat16),
            pltpu.VMEM((6, 16, 8, 128), f32),
            pltpu.VMEM((16, 8, 128), f32),
            pltpu.VMEM((16, 8, 128), f32),
            pltpu.VMEM((3, 4, 8, 128), f32),
            pltpu.VMEM((3, 16, 8, 128), f32),
            pltpu.VMEM((3, 16, 8, 128), f32),
            pltpu.VMEM((3, 3, 16, 8, 128), f32),
            pltpu.VMEM((3, 4, 8, 128), f32),
            pltpu.VMEM((3, 4, 8, 128), f32),
            pltpu.VMEM((5, 128, 128), f32),
            pltpu.VMEM((3, 128, 128), f32),
            pltpu.VMEM((3, 128, 128), f32),
            pltpu.VMEM((3, 2, 5, 8, 128), f32),
            pltpu.VMEM((3, 2, 8, 128), f32),
            pltpu.VMEM((3, 2, 5, 8, 128), f32),
            pltpu.VMEM((3, 6, 2, 8, 128), f32),
            pltpu.VMEM((3, 2, 4, 16, 128), f32),
            pltpu.SemaphoreType.DMA((7,)),
            pltpu.SemaphoreType.DMA((3, 2)),
            pltpu.SemaphoreType.DMA((3, 2)),
            pltpu.SemaphoreType.DMA((3, 6)),
            pltpu.SemaphoreType.DMA((3, 6)),
            pltpu.SemaphoreType.DMA((3, 2)),
            pltpu.SemaphoreType.DMA((3, 2)),
        ],
        compiler_params=pltpu.CompilerParams(collective_id=0, has_side_effects=True),
        name="solve",
    )(
        jnp.swapaxes(right_side, 1, 2),
        geometry.reshape(6, 16, 8, 128),
        viscosity.reshape(16, 8, 128),
        eig_low,
        eig_high,
        element_slot,
        dirichlet,
        jnp.asarray(lane_table()),
        jnp.asarray(lane_matrices()),
    )
    slots = pl.pallas_call(
        to_slots,
        out_shape=jax.ShapeDtypeStruct((3, 32, 512), f32),
        in_specs=[vmem, vmem],
        out_specs=vmem,
        name="to_slots", compiler_params=pltpu.CompilerParams(vmem_limit_bytes=8 << 20),
    )(field.reshape(3, 16, 8, 128), place)
    return jnp.swapaxes(slots, 1, 2)


def solution(mesh):
    sizes = tuple(mesh.shape[axis] for axis in ("gx", "gy", "gz"))
    return jax.shard_map(
        functools.partial(shards, sizes),
        mesh=mesh,
        in_specs=(
            P(None, None, ("gx", "gy", "gz")),
            P(None, "gx", "gy", "gz"),
            P("gx", "gy", "gz"),
            P(),
            P(),
            P(("gx", "gy", "gz"), None),
            P(None, None, "gy", "gz"),
        ),
        out_specs=P(None, None, ("gx", "gy", "gz")),
        check_vma=False,
    )
```

```python
import functools

import jax
import jax.numpy as jnp
import numpy as np
from jax import lax
from jax.experimental import pallas as pl
from jax.experimental.pallas import tpu as pltpu
from jax.sharding import PartitionSpec as P

DEGREE = 7
HELM = 10.0
N_FIRST = 5
MESH = pl.DeviceIdType.MESH

SIDES = ((-1, 0), (1, 0), (0, -1), (0, 1), (-1, -1), (-1, 1), (1, -1), (1, 1))


def legendre_pair(values, degree):
    previous = 0.0 * values + 1.0
    current = values.copy()
    for order in range(2, degree + 1):
        previous, current = (
            current,
            ((2 * order - 1) * values * current - (order - 1) * previous) / order,
        )
    return (current, previous)


def gll_tables(degree):
    start = np.cos(np.pi * np.arange(degree + 1) / degree)
    nodes_now = start.copy()
    for sweep in range(80):
        top_value, lower_value = legendre_pair(nodes_now, degree)
        nodes_now = nodes_now - (nodes_now * top_value - lower_value) / ((degree + 1) * top_value)
    gll_nodes = nodes_now[::-1].copy()
    gll_nodes[0] = -1.0
    gll_nodes[degree] = 1.0
    legendre_values = legendre_pair(gll_nodes, degree)[0]
    weights = 2.0 / (degree * (degree + 1) * legendre_values**2)
    differences = gll_nodes[:, None] - gll_nodes[None, :] + np.eye(degree + 1)
    derivative = legendre_values[:, None] / legendre_values[None, :] / differences
    derivative = derivative * (1.0 - np.eye(degree + 1))
    derivative[0, 0] = -degree * (degree + 1) / 4.0
    derivative[degree, degree] = degree * (degree + 1) / 4.0
    return (weights, derivative)


WEIGHTS, DERIVATIVE = gll_tables(DEGREE)
DF = DERIVATIVE.astype(np.float32)
WF = WEIGHTS.astype(np.float32)
DS = DF * DF
ENDS = np.diagonal(DF)


def lane_table():
    sub = np.arange(8)
    tiles = []
    for matrix in (DF, DF.T, DS.T):
        for turn in range(8):
            tiles.append(np.repeat(matrix[sub, (sub - turn) % 8][:, None], 128, axis=1))
    lane = np.arange(128) % 8
    tiles.append(WF[:, None] * WF[lane][None, :])
    tiles.append(2.0 * ENDS[:, None] * ENDS[lane][None, :])
    tiles.append(np.repeat(2.0 * ENDS[:, None], 128, axis=1))
    tiles.append(np.repeat(2.0 * ENDS[lane][None, :], 8, axis=0))
    return np.stack(tiles).astype(np.float32)


def lane_matrices():
    import ml_dtypes

    out = []
    for matrix in (DF.T, DF, DS):
        wide = np.kron(np.eye(16, dtype=np.float32), matrix).astype(np.float32)
        high = wide.astype(ml_dtypes.bfloat16)
        low = (wide - high.astype(np.float32)).astype(ml_dtypes.bfloat16)
        half = np.concatenate([high, low], axis=1)
        out.append(np.concatenate([half, half], axis=0))
    return np.stack(out)


def halves(x):
    high = x.astype(jnp.bfloat16)
    low = (x - high.astype(jnp.float32)).astype(jnp.bfloat16)
    return high, low


def slot_matrix(slot):
    row = lax.broadcasted_iota(jnp.int32, (32, 32), 0)
    element = (row & 16) + ((16 - (row & 15)) & 15)
    return jnp.where(jnp.broadcast_to(slot, (32, 32)) == element, 1.0, 0.0).astype(jnp.float32)


def turn_columns(a, b, down):
    sub = lax.broadcasted_iota(jnp.int32, (8, 128), 0)
    group = lax.broadcasted_iota(jnp.int32, (8, 128), 1) // 8
    start = (sub - group if down else sub + group) & 15
    straight = start < 8
    low, high = [], []
    for n in range(a.shape[0]):
        ta = jnp.take_along_axis(a[n], start & 7, axis=0, mode="promise_in_bounds")
        tb = jnp.take_along_axis(b[n], start & 7, axis=0, mode="promise_in_bounds")
        low.append(jnp.where(straight, ta, tb))
        high.append(jnp.where(straight, tb, ta))
    return jnp.stack(low), jnp.stack(high)


def lane_turn(x, left):
    if not left:
        return pltpu.roll(x, 0, 1, stride=8, stride_axis=0)
    row = lax.broadcasted_iota(jnp.int32, x.shape, 0)
    lane = lax.broadcasted_iota(jnp.int32, x.shape, 1)
    source = (lane + 8 * (row & 15)) & 127
    return jnp.take_along_axis(x, source, axis=1, mode="promise_in_bounds")


def along_first(matrix, planes, outs=range(8)):
    out = []
    for a in outs:
        total = None
        for i, plane in planes.items():
            if abs(matrix[a, i]) > 0:
                term = plane * float(matrix[a, i])
                total = term if total is None else total + term
        out.append(total)
    return jnp.concatenate(out, axis=0)


def mirrored(matrix, sign, field):
    wide = np.asarray(matrix, np.float64)
    planes = planes_of(field)
    even = [planes[i] + planes[7 - i] for i in range(4)]
    odd = [planes[i] - planes[7 - i] for i in range(4)]
    first, last = [], []
    for a in range(4):
        parts = []
        for terms, flip in ((even, 1.0), (odd, -1.0)):
            total = None
            for i in range(4):
                term = terms[i] * float(0.5 * (wide[a, i] + flip * wide[a, 7 - i]))
                total = term if total is None else total + term
            parts.append(total)
        first.append(parts[0] + parts[1])
        last.append((parts[0] - parts[1]) if sign > 0 else (parts[1] - parts[0]))
    return jnp.concatenate(first + last[::-1], axis=0)


def planes_of(field, first=0):
    return {first + i: field[2 * i : 2 * i + 2] for i in range(field.shape[0] // 2)}


def along_second(tab, base, field):
    total = field * tab[base]
    for turn in range(1, 8):
        total = total + pltpu.roll(field, turn, 1) * tab[base + turn]
    return total


def along_third(matrix, field):
    high, low = halves(field.reshape(-1, 128))
    both = jnp.dot(
        jnp.concatenate([high, low], axis=1), matrix, preferred_element_type=jnp.float32
    )
    return (both[:, :128] + both[:, 128:]).reshape(field.shape)


def fold_lanes(field):
    lane = lax.broadcasted_iota(jnp.int32, field.shape, 2)
    upper = (lane % 8 == 7) & (lane < 127)
    lower = (lane % 8 == 0) & (lane > 0)
    return (
        field
        + jnp.where(upper, pltpu.roll(field, 127, 2), 0.0)
        + jnp.where(lower, pltpu.roll(field, 1, 2), 0.0)
    )


def kernel(
    sizes,
    rs_h, geo_h, vis_h, low_s, high_s, slot_h, dir_h, tab_h, mat_h,
    out, place,
    rs, geo, vis, slot, dirs, tab, mats, gw, mass, inv, scale, zed, way, flux, edge, total,
    v0, v1, v2, ysend, zsend, yrecv, zrecv, xrecv,
    in_sem, ysem, yrsem, zsem, zrsem, xsem, xrsem,
):
    n_gx, n_gy, n_gz = sizes
    gx, gy, gz = lax.axis_index("gx"), lax.axis_index("gy"), lax.axis_index("gz")

    loads = [
        pltpu.make_async_copy(src, dst, in_sem.at[k])
        for k, (src, dst) in enumerate(
            (
                (rs_h, rs),
                (slot_h, slot),
                (geo_h, geo),
                (vis_h, vis),
                (tab_h, tab),
                (mat_h, mats),
                (dir_h, dirs),
            )
        )
    ]
    for load in loads:
        load.start()

    def inside(step_y, step_z):
        ok = None
        for step, at, size in ((step_y, gy, n_gy), (step_z, gz, n_gz)):
            if step:
                here = (at + step >= 0) & (at + step < size)
                ok = here if ok is None else ok & here
        return ok

    def device(step_y, step_z):
        return {"gx": gx, "gy": gy + step_y, "gz": gz + step_z}

    yrecv[...] = jnp.zeros_like(yrecv)
    zrecv[...] = jnp.zeros_like(zrecv)
    xrecv[...] = jnp.zeros_like(xrecv)

    barrier = pltpu.get_barrier_semaphore()
    count = 0
    for step_y, step_z in SIDES:
        here = inside(step_y, step_z)
        count = count + jnp.where(here, 1, 0)

        @pl.when(here)
        def _():
            pl.semaphore_signal(
                barrier, inc=1, device_id=device(step_y, step_z), device_id_type=MESH
            )

    for step in (-1, 1):
        here = (gx + step >= 0) & (gx + step < n_gx)
        count = count + jnp.where(here, 1, 0)

        @pl.when(here)
        def _():
            pl.semaphore_signal(
                barrier,
                inc=1,
                device_id={"gx": gx + step, "gy": gy, "gz": gz},
                device_id_type=MESH,
            )

    def side_copy(rnd, side, fields):
        step_y, step_z = SIDES[side]
        back = SIDES.index((-step_y, -step_z))
        if side < 2:
            part = (pl.ds(0, fields),)
            return lambda to: pltpu.make_async_remote_copy(
                src_ref=ysend.at[(rnd, side) + part],
                dst_ref=yrecv.at[(rnd, back if to else side) + part],
                send_sem=ysem.at[rnd, side],
                recv_sem=yrsem.at[rnd, back if to else side],
                device_id=device(step_y, step_z),
                device_id_type=MESH,
            )
        part = (pl.ds(0, 2 if fields > 3 else 1),)
        return lambda to: pltpu.make_async_remote_copy(
            src_ref=zsend.at[(rnd,) + part],
            dst_ref=zrecv.at[(rnd, (back if to else side) - 2) + part],
            send_sem=zsem.at[rnd, side - 2],
            recv_sem=zrsem.at[rnd, (back if to else side) - 2],
            device_id=device(step_y, step_z),
            device_id_type=MESH,
        )

    def first_copy(rnd, v, side, fields, to):
        step = (-1, 1)[side]
        plane = (0, 112)[side]
        return pltpu.make_async_remote_copy(
            src_ref=v.at[pl.ds(0, fields), pl.ds(plane, 16)],
            dst_ref=xrecv.at[rnd, (1 - side) if to else side, pl.ds(0, fields)],
            send_sem=xsem.at[rnd, side],
            recv_sem=xrsem.at[rnd, (1 - side) if to else side],
            device_id={"gx": gx + step, "gy": gy, "gz": gz},
            device_id_type=MESH,
        )

    def packed(v, fields):
        lane = lax.broadcasted_iota(jnp.int32, (8, 128), 1) // 2
        groups = [[(f, t) for f in range(3) for t in range(16)]]
        if fields > 3:
            groups.append([(3, t) for t in range(16)] + [(4, t) for t in range(6)])
        for n, group in enumerate(groups):
            parts = [None] * 4
            for q, (f, t) in enumerate(group):
                moved = pltpu.roll(v[f, pl.ds(8 * t, 8), :], 2 * q + 1, 1)
                old = parts[q % 4]
                parts[q % 4] = moved if old is None else jnp.where(lane == q, moved, old)
            for k in range(1, 4):
                parts[0] = jnp.where(lane % 4 == k, parts[k], parts[0])
            yield n, group, parts[0]

    def exchange(rnd, v, fields, x_fields):
        for f in range(fields):
            row7, row8 = v[f, pl.ds(7, 8, stride=16), :], v[f, pl.ds(8, 8, stride=16), :]
            v[f, pl.ds(7, 8, stride=16), :] = row7 + row8
            v[f, pl.ds(8, 8, stride=16), :] = row7 + row8
            ysend[rnd, 0, f] = v[f, pl.ds(0, 8, stride=16), :]
            ysend[rnd, 1, f] = v[f, pl.ds(15, 8, stride=16), :]
        if rnd == 0:
            pl.semaphore_wait(barrier, count)
        for side in (0, 1):

            @pl.when(inside(*SIDES[side]))
            def _():
                side_copy(rnd, side, fields)(True).start()

        groups = []
        for n, group, tile in packed(v, fields):
            zsend[rnd, n] = tile
            groups.append(group)
        for side in (4, 5, 6, 7, 2, 3):

            @pl.when(inside(*SIDES[side]))
            def _():
                side_copy(rnd, side, fields)(True).start()

        for side, (step_y, step_z) in enumerate(SIDES):

            @pl.when(inside(step_y, step_z))
            def _():
                side_copy(rnd, side, fields)(False).wait_recv()

        lane = lax.broadcasted_iota(jnp.int32, (8, 128), 1)
        sub = lax.broadcasted_iota(jnp.int32, (8, 128), 0)
        odd = lane % 2 == 1
        rim = (lane == 0) | (lane == 127)

        def swapped(minus, plus):
            return jnp.where(odd, pltpu.roll(minus, 1, 1), pltpu.roll(plus, 127, 1))

        for f in range(fields):
            for side, row in ((0, 0), (1, 15)):
                rows = pl.ds(row, 8, stride=16)
                v[f, rows, :] = v[f, rows, :] + yrecv[rnd, side, f]
        nears = []
        for n, group in enumerate(groups):
            near = swapped(zrecv[rnd, 0, n], zrecv[rnd, 1, n])
            below = swapped(zrecv[rnd, 2, n], zrecv[rnd, 3, n])
            above = swapped(zrecv[rnd, 4, n], zrecv[rnd, 5, n])
            below = pltpu.roll(pltpu.roll(below, 1, 0), 126, 1)
            above = pltpu.roll(pltpu.roll(above, 7, 0), 2, 1)
            upper_tile = (lane // 2) % 2 == 1
            near = near + jnp.where((sub == 0) & ~upper_tile, below, 0.0)
            nears.append(near + jnp.where((sub == 7) & upper_tile, above, 0.0))

        def unpack(wanted):
            for near, group in zip(nears, groups):
                for q, (f, t) in enumerate(group):
                    if (t in (0, 1, 14, 15) and f < 4) == wanted:
                        moved = pltpu.roll(near, (128 - (2 * q + 1)) % 128, 1)
                        tile = pl.ds(8 * t, 8)
                        v[f, tile, :] = v[f, tile, :] + jnp.where(rim, moved, 0.0)

        unpack(True)
        for side, step in enumerate((-1, 1)):

            @pl.when((gx + step >= 0) & (gx + step < n_gx))
            def _():
                first_copy(rnd, v, side, x_fields, True).start()

        unpack(False)

    def arrive(rnd, v, x_fields):
        for side, step in enumerate((-1, 1)):

            @pl.when((gx + step >= 0) & (gx + step < n_gx))
            def _():
                first_copy(rnd, v, side, x_fields, False).wait_recv()

    inner = pl.ds(2, 12)

    def middle_of(v, f):
        return v[f, pl.ds(16, 96), :].reshape(12, 8, 128)

    def rims_of(rnd, v, f):
        first = v[f, pl.ds(0, 16), :] + xrecv[rnd, 0, f]
        last = v[f, pl.ds(112, 16), :] + xrecv[rnd, 1, f]
        return jnp.concatenate([first.reshape(2, 8, 128), last.reshape(2, 8, 128)], axis=0)

    def put_rims(ref, c, value):
        ref[c, pl.ds(0, 2)] = value[:2]
        ref[c, pl.ds(14, 2)] = value[2:]

    def get_rims(ref, c):
        return jnp.concatenate([ref[c, pl.ds(0, 2)], ref[c, pl.ds(14, 2)]], axis=0)

    def fluxes(c, where, slopes, base=None):
        s1, s2, s3 = slopes
        for k, (a, b, d) in enumerate(((0, 3, 4), (3, 1, 5), (4, 5, 2))):
            flux[c, k, where] = gw[a, where] * s1 + gw[b, where] * s2 + gw[d, where] * s3

    def ahead(c):
        field = way[c, inner]
        planes = planes_of(field, 1)
        edge[c] = along_first(DF, planes, (0, 7))
        fluxes(
            c,
            inner,
            (
                along_first(DF, planes, range(1, 7)),
                along_second(tab, 0, field),
                along_third(mats[0], field),
            ),
        )

    def image_of(c):
        rims = get_rims(way, c)
        ends = {0: rims[:2], 7: rims[2:]}
        s1 = edge[c] + along_first(DF, ends, (0, 7))
        s2 = along_second(tab, 0, rims)
        s3 = along_third(mats[0], rims)
        for n, where in enumerate((pl.ds(0, 2), pl.ds(14, 2))):
            part = slice(2 * n, 2 * n + 2)
            fluxes(c, where, (s1[part], s2[part], s3[part]))
        more = along_first(DF, ends, range(1, 7))
        for k, a in enumerate((0, 3, 4)):
            flux[c, k, inner] = flux[c, k, inner] + gw[a, inner] * more
        return (
            mirrored(DF.T, -1, flux[c, 0])
            + along_second(tab, 8, flux[c, 1])
            + along_third(mats[1], flux[c, 2])
            + mass[...] * way[c]
        )

    for load in loads:
        load.wait()
    one_hot = slot_matrix(slot[...])
    place[...] = one_hot.T
    one_hot = one_hot.astype(jnp.bfloat16)
    pair = jnp.concatenate([one_hot, one_hot], axis=1)
    blocks = []
    for c in range(3):
        high, low = halves(rs[c])
        placed = jnp.dot(
            pair, jnp.concatenate([high, low], axis=0), preferred_element_type=jnp.float32
        )
        for ip in range(4):
            blocks.append(placed[:, 128 * ip : 128 * ip + 128])
    rows = lane_turn(jnp.concatenate(blocks, axis=0), True).reshape(24, 2, 8, 128)
    a, b = turn_columns(rows[:, 0], rows[:, 1], True)
    rows = jnp.stack([a, b], axis=1).reshape(384, 128)
    rows = lane_turn(rows, True).reshape(3, 4, 2, 2, 8, 128)
    for c in range(3):
        field = jnp.stack([rows[c, :, 0], rows[c, :, 1]], axis=2).reshape(16, 8, 128)
        v0[c] = fold_lanes(field).reshape(128, 128)

    quad = tab[24]
    for x in range(8):
        at = pl.ds(2 * x, 2)
        xx, yy, zz, xy, xz, yz = (geo[k, at] for k in range(6))
        quad_x = quad * float(WF[x])
        weighted = quad_x * vis[at]
        det = (
            xx * (yy * zz - yz * yz) - xy * (xy * zz - yz * xz) + xz * (xy * yz - yy * xz)
        )
        mass_x = (HELM * quad_x) * det
        mass[at] = mass_x
        for k, g in enumerate((xx, yy, zz, xy, xz, yz)):
            gw[k, at] = weighted * g
        cross = (weighted * yz) * tab[25] + mass_x
        if x in (0, 7):
            end = float(ENDS[x])
            cross = cross + (weighted * xy) * (tab[26] * end) + (weighted * xz) * (tab[27] * end)
        zed[0, at] = cross
    local = (
        mirrored(DS.T, 1, gw[0])
        + along_second(tab, 16, gw[1])
        + along_third(mats[2], gw[2])
        + zed[0]
    )
    v0[3] = fold_lanes(local).reshape(128, 128)

    low_end = jnp.where(gx == 0, 1.0, 0.0)
    high_end = jnp.where(gx == n_gx - 1, 1.0, 0.0)
    marks = dirs[0].astype(jnp.float32) * low_end + dirs[1].astype(jnp.float32) * high_end
    v0[4] = jnp.zeros((128, 128), jnp.float32)
    v0[4, :48] = fold_lanes(marks.reshape(6, 8, 128)).reshape(48, 128)

    exchange(0, v0, N_FIRST, 4)

    low = jnp.full((8, 128), low_s[0], jnp.float32)
    high = jnp.full((8, 128), high_s[0], jnp.float32)
    middle, half = (high + low) * 0.5, (high - low) * 0.5
    ratio = middle / half
    damping = 1.0 / ratio
    factors = []
    for _ in range(2):
        following = 1.0 / (2.0 * ratio - damping)
        factors.append((following * damping, 2.0 * following / half))
        damping = following

    inverse = 1.0 / middle_of(v0, 3)
    inv[inner] = inverse
    for c in range(3):
        start = inverse * middle_of(v0, c)
        zed[c, inner] = start
        way[c, inner] = start / middle
        out[c, pl.ds(16, 96), :] = way[c, inner].reshape(96, 128)
    for c in range(3):
        ahead(c)
    arrive(0, v0, 4)
    inverse = 1.0 / rims_of(0, v0, 3)
    for c in range(3):
        flags = v0[4, pl.ds(16 * c, 16), :].reshape(2, 8, 128)
        free = jnp.where(flags > 0.5, 0.0, 1.0)
        keep_low = free * low_end + (1.0 - low_end)
        keep_high = free * high_end + (1.0 - high_end)
        scale[c] = inverse * jnp.concatenate([keep_low, keep_high], axis=0)
        start = scale[c] * rims_of(0, v0, c)
        put_rims(zed, c, start)
        put_rims(way, c, start / middle)

    for rnd, v in ((1, v1), (2, v2)):
        for c in range(3):
            v[c] = fold_lanes(image_of(c)).reshape(128, 128)
        exchange(rnd, v, 3, 3)
        keep_by, add_by = factors[rnd - 1]
        for c in range(3):
            rest = zed[c, inner] - inv[inner] * middle_of(v, c)
            step = keep_by * way[c, inner] + add_by * rest
            out[c, pl.ds(16, 96), :] = out[c, pl.ds(16, 96), :] + step.reshape(96, 128)
            if rnd == 1:
                zed[c, inner] = rest
                way[c, inner] = step
        for c in range(3):
            if rnd == 1:
                ahead(c)
                total[c] = get_rims(way, c)
        arrive(rnd, v, 3)
        for c in range(3):
            rest = get_rims(zed, c) - scale[c] * rims_of(rnd, v, c)
            step = keep_by * get_rims(way, c) + add_by * rest
            if rnd == 1:
                put_rims(zed, c, rest)
                put_rims(way, c, step)
            total[c] = total[c] + step
            if rnd == 2:
                whole = total[c].reshape(32, 128)
                out[c, pl.ds(0, 16), :] = whole[:16]
                out[c, pl.ds(112, 16), :] = whole[16:]

    for rnd, v, fields, x_fields in ((0, v0, N_FIRST, 4), (1, v1, 3, 3), (2, v2, 3, 3)):
        for side, (step_y, step_z) in enumerate(SIDES):

            @pl.when(inside(step_y, step_z))
            def _():
                side_copy(rnd, side, fields)(True).wait_send()

        for side, step in enumerate((-1, 1)):

            @pl.when((gx + step >= 0) & (gx + step < n_gx))
            def _():
                first_copy(rnd, v, side, x_fields, True).wait_send()


def to_slots(field, place, out):
    rows = field[...].reshape(3, 4, 2, 2, 8, 128)
    rows = jnp.stack([rows[:, :, 0], rows[:, :, 1]], axis=3).reshape(384, 128)
    rows = lane_turn(rows, False).reshape(24, 2, 8, 128)
    a, b = turn_columns(rows[:, 0], rows[:, 1], False)
    rows = lane_turn(jnp.stack([a, b], axis=1).reshape(384, 128), False).reshape(3, 4, 32, 128)
    one_hot = place[...].astype(jnp.bfloat16)
    pair = jnp.concatenate([one_hot, one_hot], axis=1)
    for c in range(3):
        wide = jnp.concatenate([rows[c, ip] for ip in range(4)], axis=1)
        high, low = halves(wide)
        out[c] = jnp.dot(
            pair, jnp.concatenate([high, low], axis=0), preferred_element_type=jnp.float32
        )


def shards(sizes, right_side, geometry, viscosity, eig_low, eig_high, element_slot, dirichlet):
    f32 = jnp.float32
    anywhere = pl.BlockSpec(memory_space=pl.ANY)
    scalar = pl.BlockSpec(memory_space=pltpu.SMEM)
    vmem = pl.BlockSpec(memory_space=pltpu.VMEM)
    field, place = pl.pallas_call(
        functools.partial(kernel, sizes),
        out_shape=(pltpu.VMEM((3, 128, 128), f32), pltpu.VMEM((32, 32), f32)),
        in_specs=[anywhere] * 3 + [scalar] * 2 + [anywhere] * 4,
        out_specs=(vmem, vmem),
        scratch_shapes=[
            pltpu.VMEM((3, 32, 512), f32),
            pltpu.VMEM((6, 16, 8, 128), f32),
            pltpu.VMEM((16, 8, 128), f32),
            pltpu.VMEM((1, 32), jnp.int32),
            pltpu.VMEM((2, 3, 16, 128), jnp.int32),
            pltpu.VMEM((28, 8, 128), f32),
            pltpu.VMEM((3, 256, 256), jnp.bfloat16),
            pltpu.VMEM((6, 16, 8, 128), f32),
            pltpu.VMEM((16, 8, 128), f32),
            pltpu.VMEM((16, 8, 128), f32),
            pltpu.VMEM((3, 4, 8, 128), f32),
            pltpu.VMEM((3, 16, 8, 128), f32),
            pltpu.VMEM((3, 16, 8, 128), f32),
            pltpu.VMEM((3, 3, 16, 8, 128), f32),
            pltpu.VMEM((3, 4, 8, 128), f32),
            pltpu.VMEM((3, 4, 8, 128), f32),
            pltpu.VMEM((5, 128, 128), f32),
            pltpu.VMEM((3, 128, 128), f32),
            pltpu.VMEM((3, 128, 128), f32),
            pltpu.VMEM((3, 2, 5, 8, 128), f32),
            pltpu.VMEM((3, 2, 8, 128), f32),
            pltpu.VMEM((3, 2, 5, 8, 128), f32),
            pltpu.VMEM((3, 6, 2, 8, 128), f32),
            pltpu.VMEM((3, 2, 4, 16, 128), f32),
            pltpu.SemaphoreType.DMA((7,)),
            pltpu.SemaphoreType.DMA((3, 2)),
            pltpu.SemaphoreType.DMA((3, 2)),
            pltpu.SemaphoreType.DMA((3, 6)),
            pltpu.SemaphoreType.DMA((3, 6)),
            pltpu.SemaphoreType.DMA((3, 2)),
            pltpu.SemaphoreType.DMA((3, 2)),
        ],
        compiler_params=pltpu.CompilerParams(collective_id=0, has_side_effects=True),
        name="solve",
    )(
        jnp.swapaxes(right_side, 1, 2),
        geometry.reshape(6, 16, 8, 128),
        viscosity.reshape(16, 8, 128),
        eig_low,
        eig_high,
        element_slot,
        dirichlet,
        jnp.asarray(lane_table()),
        jnp.asarray(lane_matrices()),
    )
    slots = pl.pallas_call(
        to_slots,
        out_shape=jax.ShapeDtypeStruct((3, 32, 512), f32),
        in_specs=[vmem, vmem],
        out_specs=vmem,
        name="to_slots", compiler_params=pltpu.CompilerParams(vmem_limit_bytes=8 << 20),
    )(field.reshape(3, 16, 8, 128), place)
    return jnp.swapaxes(slots, 1, 2)


def solution(mesh):
    sizes = tuple(mesh.shape[axis] for axis in ("gx", "gy", "gz"))
    return jax.shard_map(
        functools.partial(shards, sizes),
        mesh=mesh,
        in_specs=(
            P(None, None, ("gx", "gy", "gz")),
            P(None, "gx", "gy", "gz"),
            P("gx", "gy", "gz"),
            P(),
            P(),
            P(("gx", "gy", "gz"), None),
            P(None, None, "gy", "gz"),
        ),
        out_specs=P(None, None, ("gx", "gy", "gz")),
        check_vma=False,
    )
```

```python
import functools

import jax
import jax.numpy as jnp
import numpy as np
from jax import lax
from jax.experimental import pallas as pl
from jax.experimental.pallas import tpu as pltpu
from jax.sharding import PartitionSpec as P

DEGREE = 7
HELM = 10.0
N_FIRST = 5
MESH = pl.DeviceIdType.MESH

SIDES = ((-1, 0), (1, 0), (0, -1), (0, 1), (-1, -1), (-1, 1), (1, -1), (1, 1))


def legendre_pair(values, degree):
    previous = 0.0 * values + 1.0
    current = values.copy()
    for order in range(2, degree + 1):
        previous, current = (
            current,
            ((2 * order - 1) * values * current - (order - 1) * previous) / order,
        )
    return (current, previous)


def gll_tables(degree):
    start = np.cos(np.pi * np.arange(degree + 1) / degree)
    nodes_now = start.copy()
    for sweep in range(80):
        top_value, lower_value = legendre_pair(nodes_now, degree)
        nodes_now = nodes_now - (nodes_now * top_value - lower_value) / ((degree + 1) * top_value)
    gll_nodes = nodes_now[::-1].copy()
    gll_nodes[0] = -1.0
    gll_nodes[degree] = 1.0
    legendre_values = legendre_pair(gll_nodes, degree)[0]
    weights = 2.0 / (degree * (degree + 1) * legendre_values**2)
    differences = gll_nodes[:, None] - gll_nodes[None, :] + np.eye(degree + 1)
    derivative = legendre_values[:, None] / legendre_values[None, :] / differences
    derivative = derivative * (1.0 - np.eye(degree + 1))
    derivative[0, 0] = -degree * (degree + 1) / 4.0
    derivative[degree, degree] = degree * (degree + 1) / 4.0
    return (weights, derivative)


ENDS_AT = (0, 1, 14, 15)

WEIGHTS, DERIVATIVE = gll_tables(DEGREE)
DF = DERIVATIVE.astype(np.float32)
WF = WEIGHTS.astype(np.float32)
DS = DF * DF
ENDS = np.diagonal(DF)


def lane_table():
    sub = np.arange(8)
    tiles = []
    for matrix in (DF, DF.T, DS.T):
        for turn in range(8):
            tiles.append(np.repeat(matrix[sub, (sub - turn) % 8][:, None], 128, axis=1))
    lane = np.arange(128) % 8
    tiles.append(WF[:, None] * WF[lane][None, :])
    tiles.append(2.0 * ENDS[:, None] * ENDS[lane][None, :])
    tiles.append(np.repeat(2.0 * ENDS[:, None], 128, axis=1))
    tiles.append(np.repeat(2.0 * ENDS[lane][None, :], 8, axis=0))
    return np.stack(tiles).astype(np.float32)


def lane_matrices():
    import ml_dtypes

    out = []
    for matrix in (DF.T, DF, DS):
        wide = np.kron(np.eye(16, dtype=np.float32), matrix).astype(np.float32)
        high = wide.astype(ml_dtypes.bfloat16)
        low = (wide - high.astype(np.float32)).astype(ml_dtypes.bfloat16)
        half = np.concatenate([high, low], axis=1)
        out.append(np.concatenate([half, half], axis=0))
    return np.stack(out)


def halves(x):
    high = x.astype(jnp.bfloat16)
    low = (x - high.astype(jnp.float32)).astype(jnp.bfloat16)
    return high, low


def slot_matrix(slot):
    row = lax.broadcasted_iota(jnp.int32, (32, 32), 0)
    element = (row & 16) + ((16 - (row & 15)) & 15)
    return jnp.where(jnp.broadcast_to(slot, (32, 32)) == element, 1.0, 0.0).astype(jnp.float32)


def turn_columns(a, b, down):
    sub = lax.broadcasted_iota(jnp.int32, (8, 128), 0)
    group = lax.broadcasted_iota(jnp.int32, (8, 128), 1) // 8
    start = (sub - group if down else sub + group) & 15
    straight = start < 8
    low, high = [], []
    for n in range(a.shape[0]):
        ta = jnp.take_along_axis(a[n], start & 7, axis=0, mode="promise_in_bounds")
        tb = jnp.take_along_axis(b[n], start & 7, axis=0, mode="promise_in_bounds")
        low.append(jnp.where(straight, ta, tb))
        high.append(jnp.where(straight, tb, ta))
    return jnp.stack(low), jnp.stack(high)


def lane_turn(x, left):
    if not left:
        return pltpu.roll(x, 0, 1, stride=8, stride_axis=0)
    row = lax.broadcasted_iota(jnp.int32, x.shape, 0)
    lane = lax.broadcasted_iota(jnp.int32, x.shape, 1)
    source = (lane + 8 * (row & 15)) & 127
    return jnp.take_along_axis(x, source, axis=1, mode="promise_in_bounds")


def along_first(matrix, planes, outs=range(8)):
    out = []
    for a in outs:
        total = None
        for i, plane in planes.items():
            if abs(matrix[a, i]) > 0:
                term = plane * float(matrix[a, i])
                total = term if total is None else total + term
        out.append(total)
    return jnp.concatenate(out, axis=0)


def planes_of(field, first=0):
    return {first + i: field[2 * i : 2 * i + 2] for i in range(field.shape[0] // 2)}


def along_second(tab, base, field):
    total = field * tab[base]
    for turn in range(1, 8):
        total = total + pltpu.roll(field, turn, 1) * tab[base + turn]
    return total


def along_third(matrix, field):
    high, low = halves(field.reshape(-1, 128))
    both = jnp.dot(
        jnp.concatenate([high, low], axis=1), matrix, preferred_element_type=jnp.float32
    )
    return (both[:, :128] + both[:, 128:]).reshape(field.shape)


def fold_lanes(field):
    lane = lax.broadcasted_iota(jnp.int32, field.shape, 2)
    upper = (lane % 8 == 7) & (lane < 127)
    lower = (lane % 8 == 0) & (lane > 0)
    return (
        field
        + jnp.where(upper, pltpu.roll(field, 127, 2), 0.0)
        + jnp.where(lower, pltpu.roll(field, 1, 2), 0.0)
    )


def kernel(
    sizes,
    rs_h, geo_h, vis_h, low_s, high_s, slot_h, dir_h, tab_h, mat_h,
    out, place,
    rs, geo, vis, slot, dirs, tab, mats, gw, mass, inv, scale, zed, way, flux, edge, total,
    v0, v1, v2, own, fsend, frecv, ysend, zsend, yrecv, zrecv, xrecv,
    in_sem, ysem, yrsem, zsem, zrsem, xsem, xrsem, fsem, frsem,
):
    n_gx, n_gy, n_gz = sizes
    gx, gy, gz = lax.axis_index("gx"), lax.axis_index("gy"), lax.axis_index("gz")

    loads = [
        pltpu.make_async_copy(src, dst, in_sem.at[k])
        for k, (src, dst) in enumerate(
            (
                (rs_h, rs),
                (slot_h, slot),
                (geo_h, geo),
                (vis_h, vis),
                (tab_h, tab),
                (mat_h, mats),
                (dir_h, dirs),
            )
        )
    ]
    for load in loads:
        load.start()

    def inside(step_y, step_z):
        ok = None
        for step, at, size in ((step_y, gy, n_gy), (step_z, gz, n_gz)):
            if step:
                here = (at + step >= 0) & (at + step < size)
                ok = here if ok is None else ok & here
        return ok

    def device(step_y, step_z):
        return {"gx": gx, "gy": gy + step_y, "gz": gz + step_z}

    yrecv[...] = jnp.zeros_like(yrecv)
    zrecv[...] = jnp.zeros_like(zrecv)
    xrecv[...] = jnp.zeros_like(xrecv)
    frecv[...] = jnp.zeros_like(frecv)
    fsend[...] = jnp.zeros_like(fsend)

    barrier = pltpu.get_barrier_semaphore()
    count = 0
    for step_y, step_z in SIDES:
        here = inside(step_y, step_z)
        count = count + jnp.where(here, 1, 0)

        @pl.when(here)
        def _():
            pl.semaphore_signal(
                barrier, inc=1, device_id=device(step_y, step_z), device_id_type=MESH
            )

    for step in (-1, 1):
        here = (gx + step >= 0) & (gx + step < n_gx)
        count = count + jnp.where(here, 1, 0)

        @pl.when(here)
        def _():
            pl.semaphore_signal(
                barrier,
                inc=1,
                device_id={"gx": gx + step, "gy": gy, "gz": gz},
                device_id_type=MESH,
            )

    def side_copy(rnd, side, fields):
        step_y, step_z = SIDES[side]
        back = SIDES.index((-step_y, -step_z))
        if side < 2:
            part = (pl.ds(0, fields),)
            return lambda to: pltpu.make_async_remote_copy(
                src_ref=ysend.at[(rnd, side) + part],
                dst_ref=yrecv.at[(rnd, back if to else side) + part],
                send_sem=ysem.at[rnd, side],
                recv_sem=yrsem.at[rnd, back if to else side],
                device_id=device(step_y, step_z),
                device_id_type=MESH,
            )
        part = (pl.ds(0, 2 if fields > 3 else 1),)
        return lambda to: pltpu.make_async_remote_copy(
            src_ref=zsend.at[(rnd,) + part],
            dst_ref=zrecv.at[(rnd, (back if to else side) - 2) + part],
            send_sem=zsem.at[rnd, side - 2],
            recv_sem=zrsem.at[rnd, (back if to else side) - 2],
            device_id=device(step_y, step_z),
            device_id_type=MESH,
        )

    def first_copy(rnd, v, side, fields, to):
        step = (-1, 1)[side]
        plane = (0, 112)[side]
        return pltpu.make_async_remote_copy(
            src_ref=v.at[pl.ds(0, fields), pl.ds(plane, 16)],
            dst_ref=xrecv.at[rnd, (1 - side) if to else side, pl.ds(0, fields)],
            send_sem=xsem.at[rnd, side],
            recv_sem=xrsem.at[rnd, (1 - side) if to else side],
            device_id={"gx": gx + step, "gy": gy, "gz": gz},
            device_id_type=MESH,
        )

    def fix_copy(rnd, side, tiles, to):
        step = (-1, 1)[side]
        return pltpu.make_async_remote_copy(
            src_ref=fsend.at[rnd, side, pl.ds(0, tiles)],
            dst_ref=frecv.at[rnd, (1 - side) if to else side, pl.ds(0, tiles)],
            send_sem=fsem.at[rnd, side],
            recv_sem=frsem.at[rnd, (1 - side) if to else side],
            device_id={"gx": gx + step, "gy": gy, "gz": gz},
            device_id_type=MESH,
        )

    def beside(side):
        return (gx + (-1, 1)[side] >= 0) & (gx + (-1, 1)[side] < n_gx)

    def packed(v, fields):
        lane = lax.broadcasted_iota(jnp.int32, (8, 128), 1) // 2
        groups = [[(f, t) for f in range(3) for t in range(16)]]
        if fields > 3:
            groups.append([(3, t) for t in range(16)] + [(4, t) for t in range(6)])
        for n, group in enumerate(groups):
            parts = [None] * 4
            for q, (f, t) in enumerate(group):
                moved = pltpu.roll(v[f, pl.ds(8 * t, 8), :], 2 * q + 1, 1)
                old = parts[q % 4]
                parts[q % 4] = moved if old is None else jnp.where(lane == q, moved, old)
            for k in range(1, 4):
                parts[0] = jnp.where(lane % 4 == k, parts[k], parts[0])
            yield n, group, parts[0]

    def exchange(rnd, v, fields, x_fields):
        for f in range(fields):
            row7, row8 = v[f, pl.ds(7, 8, stride=16), :], v[f, pl.ds(8, 8, stride=16), :]
            v[f, pl.ds(7, 8, stride=16), :] = row7 + row8
            v[f, pl.ds(8, 8, stride=16), :] = row7 + row8
            ysend[rnd, 0, f] = v[f, pl.ds(0, 8, stride=16), :]
            ysend[rnd, 1, f] = v[f, pl.ds(15, 8, stride=16), :]
        if rnd == 0:
            pl.semaphore_wait(barrier, count)
        for side in (0, 1):

            @pl.when(inside(*SIDES[side]))
            def _():
                side_copy(rnd, side, fields)(True).start()

        groups = []
        for n, group, tile in packed(v, fields):
            zsend[rnd, n] = tile
            groups.append(group)
        for side in (4, 5, 6, 7, 2, 3):

            @pl.when(inside(*SIDES[side]))
            def _():
                side_copy(rnd, side, fields)(True).start()

        for side in (0, 1):

            @pl.when(beside(side))
            def _():
                first_copy(rnd, v, side, x_fields, True).start()

        for side, (step_y, step_z) in enumerate(SIDES):

            @pl.when(inside(step_y, step_z))
            def _():
                side_copy(rnd, side, fields)(False).wait_recv()

        lane = lax.broadcasted_iota(jnp.int32, (8, 128), 1)
        sub = lax.broadcasted_iota(jnp.int32, (8, 128), 0)
        odd = lane % 2 == 1
        rim = (lane == 0) | (lane == 127)

        def swapped(minus, plus):
            return jnp.where(odd, pltpu.roll(minus, 1, 1), pltpu.roll(plus, 127, 1))

        nears = []
        for n, group in enumerate(groups):
            near = swapped(zrecv[rnd, 0, n], zrecv[rnd, 1, n])
            below = swapped(zrecv[rnd, 2, n], zrecv[rnd, 3, n])
            above = swapped(zrecv[rnd, 4, n], zrecv[rnd, 5, n])
            below = pltpu.roll(pltpu.roll(below, 1, 0), 126, 1)
            above = pltpu.roll(pltpu.roll(above, 7, 0), 2, 1)
            upper_tile = (lane // 2) % 2 == 1
            near = near + jnp.where((sub == 0) & ~upper_tile, below, 0.0)
            nears.append(near + jnp.where((sub == 7) & upper_tile, above, 0.0))

        tiles = len(groups) + 1
        for side in (0, 1):
            for n, near in enumerate(nears):
                fsend[rnd, side, n] = near
            for f in range(x_fields):
                for y_side in (0, 1):
                    fsend[rnd, side, tiles - 1, pl.ds(2 * f + y_side, 1), :] = yrecv[
                        rnd, y_side, f, pl.ds(7 * side, 1), :
                    ]

            @pl.when(beside(side))
            def _():
                fix_copy(rnd, side, tiles, True).start()

        for near, group in zip(nears, groups):
            for q, (f, t) in enumerate(group):
                added = jnp.where(rim, pltpu.roll(near, (128 - (2 * q + 1)) % 128, 1), 0.0)
                value = v[f, pl.ds(8 * t, 8), :] + added
                if f < 4 and t in ENDS_AT:
                    own[f, ENDS_AT.index(t)] = value
                else:
                    v[f, pl.ds(8 * t, 8), :] = value
        for f in range(fields):
            for side, row in ((0, 0), (1, 15)):
                if f < 4:
                    rows = pl.ds(16 + row, 6, stride=16)
                    v[f, rows, :] = v[f, rows, :] + yrecv[rnd, side, f, pl.ds(1, 6), :]
                    at = pl.ds(7 * side, 1)
                    for x, tile in ((0, side), (7, 2 + side)):
                        own[f, tile, at, :] = own[f, tile, at, :] + yrecv[rnd, side, f, pl.ds(x, 1), :]
                else:
                    rows = pl.ds(row, 8, stride=16)
                    v[f, rows, :] = v[f, rows, :] + yrecv[rnd, side, f]

    def arrive(rnd, v, x_fields):
        for side in (0, 1):

            @pl.when(beside(side))
            def _():
                first_copy(rnd, v, side, x_fields, False).wait_recv()
                fix_copy(rnd, side, 3 if x_fields > 3 else 2, False).wait_recv()

    inner = pl.ds(2, 12)

    def middle_of(v, f):
        return v[f, pl.ds(16, 96), :].reshape(12, 8, 128)

    def rims_of(rnd, v, f):
        lane = lax.broadcasted_iota(jnp.int32, (8, 128), 1)
        sub = lax.broadcasted_iota(jnp.int32, (8, 128), 0)
        last = 2 if rnd == 0 else 1
        out = []
        for k, t in enumerate((14, 15, 0, 1)):
            side, half = k // 2, k % 2
            q = 16 * (f % 3) + t
            moved = pltpu.roll(frecv[rnd, side, f // 3], (128 - (2 * q + 1)) % 128, 1)
            row = jnp.broadcast_to(frecv[rnd, side, last, pl.ds(2 * f + half, 1), :], (8, 128))
            out.append(
                own[f, k]
                + xrecv[rnd, side, f, pl.ds(8 * half, 8), :]
                + jnp.where((lane == 0) | (lane == 127), moved, 0.0)
                + jnp.where(sub == 7 * half, row, 0.0)
            )
        return jnp.stack(out)

    def put_rims(ref, c, value):
        ref[c, pl.ds(0, 2)] = value[:2]
        ref[c, pl.ds(14, 2)] = value[2:]

    def get_rims(ref, c):
        return jnp.concatenate([ref[c, pl.ds(0, 2)], ref[c, pl.ds(14, 2)]], axis=0)

    def fluxes(c, where, slopes, base=None):
        s1, s2, s3 = slopes
        for k, (a, b, d) in enumerate(((0, 3, 4), (3, 1, 5), (4, 5, 2))):
            flux[c, k, where] = gw[a, where] * s1 + gw[b, where] * s2 + gw[d, where] * s3

    def ahead(c):
        field = way[c, inner]
        planes = planes_of(field, 1)
        edge[c] = along_first(DF, planes, (0, 7))
        fluxes(
            c,
            inner,
            (
                along_first(DF, planes, range(1, 7)),
                along_second(tab, 0, field),
                along_third(mats[0], field),
            ),
        )

    def image_of(c):
        rims = get_rims(way, c)
        ends = {0: rims[:2], 7: rims[2:]}
        s1 = edge[c] + along_first(DF, ends, (0, 7))
        s2 = along_second(tab, 0, rims)
        s3 = along_third(mats[0], rims)
        for n, where in enumerate((pl.ds(0, 2), pl.ds(14, 2))):
            part = slice(2 * n, 2 * n + 2)
            fluxes(c, where, (s1[part], s2[part], s3[part]))
        more = along_first(DF, ends, range(1, 7))
        for k, a in enumerate((0, 3, 4)):
            flux[c, k, inner] = flux[c, k, inner] + gw[a, inner] * more
        return (
            along_first(DF.T, planes_of(flux[c, 0]))
            + along_second(tab, 8, flux[c, 1])
            + along_third(mats[1], flux[c, 2])
            + mass[...] * way[c]
        )

    loads[0].wait()
    loads[1].wait()
    one_hot = slot_matrix(slot[...])
    place[...] = one_hot.T
    one_hot = one_hot.astype(jnp.bfloat16)
    pair = jnp.concatenate([one_hot, one_hot], axis=1)
    blocks = []
    for c in range(3):
        high, low = halves(rs[c])
        placed = jnp.dot(
            pair, jnp.concatenate([high, low], axis=0), preferred_element_type=jnp.float32
        )
        for ip in range(4):
            blocks.append(placed[:, 128 * ip : 128 * ip + 128])
    rows = lane_turn(jnp.concatenate(blocks, axis=0), True).reshape(24, 2, 8, 128)
    a, b = turn_columns(rows[:, 0], rows[:, 1], True)
    rows = jnp.stack([a, b], axis=1).reshape(384, 128)
    rows = lane_turn(rows, True).reshape(3, 4, 2, 2, 8, 128)
    for c in range(3):
        field = jnp.stack([rows[c, :, 0], rows[c, :, 1]], axis=2).reshape(16, 8, 128)
        v0[c] = fold_lanes(field).reshape(128, 128)

    for load in loads[2:]:
        load.wait()

    quad = tab[24]
    for x in range(8):
        at = pl.ds(2 * x, 2)
        xx, yy, zz, xy, xz, yz = (geo[k, at] for k in range(6))
        quad_x = quad * float(WF[x])
        weighted = quad_x * vis[at]
        det = (
            xx * (yy * zz - yz * yz) - xy * (xy * zz - yz * xz) + xz * (xy * yz - yy * xz)
        )
        mass_x = (HELM * quad_x) * det
        mass[at] = mass_x
        for k, g in enumerate((xx, yy, zz, xy, xz, yz)):
            gw[k, at] = weighted * g
        cross = (weighted * yz) * tab[25] + mass_x
        if x in (0, 7):
            end = float(ENDS[x])
            cross = cross + (weighted * xy) * (tab[26] * end) + (weighted * xz) * (tab[27] * end)
        zed[0, at] = cross
    local = (
        along_first(DS.T, planes_of(gw[0]))
        + along_second(tab, 16, gw[1])
        + along_third(mats[2], gw[2])
        + zed[0]
    )
    v0[3] = fold_lanes(local).reshape(128, 128)

    low_end = jnp.where(gx == 0, 1.0, 0.0)
    high_end = jnp.where(gx == n_gx - 1, 1.0, 0.0)
    marks = dirs[0].astype(jnp.float32) * low_end + dirs[1].astype(jnp.float32) * high_end
    v0[4] = jnp.zeros((128, 128), jnp.float32)
    v0[4, :48] = fold_lanes(marks.reshape(6, 8, 128)).reshape(48, 128)

    exchange(0, v0, N_FIRST, 4)

    low = jnp.full((8, 128), low_s[0], jnp.float32)
    high = jnp.full((8, 128), high_s[0], jnp.float32)
    middle, half = (high + low) * 0.5, (high - low) * 0.5
    ratio = middle / half
    damping = 1.0 / ratio
    factors = []
    for _ in range(2):
        following = 1.0 / (2.0 * ratio - damping)
        factors.append((following * damping, 2.0 * following / half))
        damping = following

    inverse = 1.0 / middle_of(v0, 3)
    inv[inner] = inverse
    for c in range(3):
        start = inverse * middle_of(v0, c)
        zed[c, inner] = start
        way[c, inner] = start / middle
        out[c, pl.ds(16, 96), :] = way[c, inner].reshape(96, 128)
    for c in range(3):
        ahead(c)
    arrive(0, v0, 4)
    inverse = 1.0 / rims_of(0, v0, 3)
    for c in range(3):
        flags = v0[4, pl.ds(16 * c, 16), :].reshape(2, 8, 128)
        free = jnp.where(flags > 0.5, 0.0, 1.0)
        keep_low = free * low_end + (1.0 - low_end)
        keep_high = free * high_end + (1.0 - high_end)
        scale[c] = inverse * jnp.concatenate([keep_low, keep_high], axis=0)
        start = scale[c] * rims_of(0, v0, c)
        put_rims(zed, c, start)
        put_rims(way, c, start / middle)

    for rnd, v in ((1, v1), (2, v2)):
        for c in range(3):
            v[c] = fold_lanes(image_of(c)).reshape(128, 128)
        exchange(rnd, v, 3, 3)
        keep_by, add_by = factors[rnd - 1]
        for c in range(3):
            rest = zed[c, inner] - inv[inner] * middle_of(v, c)
            step = keep_by * way[c, inner] + add_by * rest
            out[c, pl.ds(16, 96), :] = out[c, pl.ds(16, 96), :] + step.reshape(96, 128)
            if rnd == 1:
                zed[c, inner] = rest
                way[c, inner] = step
        for c in range(3):
            if rnd == 1:
                ahead(c)
                total[c] = get_rims(way, c)
        arrive(rnd, v, 3)
        for c in range(3):
            rest = get_rims(zed, c) - scale[c] * rims_of(rnd, v, c)
            step = keep_by * get_rims(way, c) + add_by * rest
            if rnd == 1:
                put_rims(zed, c, rest)
                put_rims(way, c, step)
            total[c] = total[c] + step
            if rnd == 2:
                whole = total[c].reshape(32, 128)
                out[c, pl.ds(0, 16), :] = whole[:16]
                out[c, pl.ds(112, 16), :] = whole[16:]

    for rnd, v, fields, x_fields in ((0, v0, N_FIRST, 4), (1, v1, 3, 3), (2, v2, 3, 3)):
        for side, (step_y, step_z) in enumerate(SIDES):

            @pl.when(inside(step_y, step_z))
            def _():
                side_copy(rnd, side, fields)(True).wait_send()

        for side, step in enumerate((-1, 1)):

            @pl.when((gx + step >= 0) & (gx + step < n_gx))
            def _():
                first_copy(rnd, v, side, x_fields, True).wait_send()
                fix_copy(rnd, side, 3 if x_fields > 3 else 2, True).wait_send()


def to_slots(field, place, out):
    rows = field[...].reshape(3, 4, 2, 2, 8, 128)
    rows = jnp.stack([rows[:, :, 0], rows[:, :, 1]], axis=3).reshape(384, 128)
    rows = lane_turn(rows, False).reshape(24, 2, 8, 128)
    a, b = turn_columns(rows[:, 0], rows[:, 1], False)
    rows = lane_turn(jnp.stack([a, b], axis=1).reshape(384, 128), False).reshape(3, 4, 32, 128)
    one_hot = place[...].astype(jnp.bfloat16)
    pair = jnp.concatenate([one_hot, one_hot], axis=1)
    for c in range(3):
        wide = jnp.concatenate([rows[c, ip] for ip in range(4)], axis=1)
        high, low = halves(wide)
        out[c] = jnp.dot(
            pair, jnp.concatenate([high, low], axis=0), preferred_element_type=jnp.float32
        )


def shards(sizes, right_side, geometry, viscosity, eig_low, eig_high, element_slot, dirichlet):
    f32 = jnp.float32
    anywhere = pl.BlockSpec(memory_space=pl.ANY)
    scalar = pl.BlockSpec(memory_space=pltpu.SMEM)
    vmem = pl.BlockSpec(memory_space=pltpu.VMEM)
    field, place = pl.pallas_call(
        functools.partial(kernel, sizes),
        out_shape=(pltpu.VMEM((3, 128, 128), f32), pltpu.VMEM((32, 32), f32)),
        in_specs=[anywhere] * 3 + [scalar] * 2 + [anywhere] * 4,
        out_specs=(vmem, vmem),
        scratch_shapes=[
            pltpu.VMEM((3, 32, 512), f32),
            pltpu.VMEM((6, 16, 8, 128), f32),
            pltpu.VMEM((16, 8, 128), f32),
            pltpu.VMEM((1, 32), jnp.int32),
            pltpu.VMEM((2, 3, 16, 128), jnp.int32),
            pltpu.VMEM((28, 8, 128), f32),
            pltpu.VMEM((3, 256, 256), jnp.bfloat16),
            pltpu.VMEM((6, 16, 8, 128), f32),
            pltpu.VMEM((16, 8, 128), f32),
            pltpu.VMEM((16, 8, 128), f32),
            pltpu.VMEM((3, 4, 8, 128), f32),
            pltpu.VMEM((3, 16, 8, 128), f32),
            pltpu.VMEM((3, 16, 8, 128), f32),
            pltpu.VMEM((3, 3, 16, 8, 128), f32),
            pltpu.VMEM((3, 4, 8, 128), f32),
            pltpu.VMEM((3, 4, 8, 128), f32),
            pltpu.VMEM((5, 128, 128), f32),
            pltpu.VMEM((3, 128, 128), f32),
            pltpu.VMEM((3, 128, 128), f32),
            pltpu.VMEM((4, 4, 8, 128), f32),
            pltpu.VMEM((3, 2, 3, 8, 128), f32),
            pltpu.VMEM((3, 2, 3, 8, 128), f32),
            pltpu.VMEM((3, 2, 5, 8, 128), f32),
            pltpu.VMEM((3, 2, 8, 128), f32),
            pltpu.VMEM((3, 2, 5, 8, 128), f32),
            pltpu.VMEM((3, 6, 2, 8, 128), f32),
            pltpu.VMEM((3, 2, 4, 16, 128), f32),
            pltpu.SemaphoreType.DMA((7,)),
            pltpu.SemaphoreType.DMA((3, 2)),
            pltpu.SemaphoreType.DMA((3, 2)),
            pltpu.SemaphoreType.DMA((3, 6)),
            pltpu.SemaphoreType.DMA((3, 6)),
            pltpu.SemaphoreType.DMA((3, 2)),
            pltpu.SemaphoreType.DMA((3, 2)),
            pltpu.SemaphoreType.DMA((3, 2)),
            pltpu.SemaphoreType.DMA((3, 2)),
        ],
        compiler_params=pltpu.CompilerParams(collective_id=0, has_side_effects=True),
        name="solve",
    )(
        jnp.swapaxes(right_side, 1, 2),
        geometry.reshape(6, 16, 8, 128),
        viscosity.reshape(16, 8, 128),
        eig_low,
        eig_high,
        element_slot,
        dirichlet,
        jnp.asarray(lane_table()),
        jnp.asarray(lane_matrices()),
    )
    slots = pl.pallas_call(
        to_slots,
        out_shape=jax.ShapeDtypeStruct((3, 32, 512), f32),
        in_specs=[vmem, vmem],
        out_specs=vmem,
        name="to_slots", compiler_params=pltpu.CompilerParams(vmem_limit_bytes=8 << 20),
    )(field.reshape(3, 16, 8, 128), place)
    return jnp.swapaxes(slots, 1, 2)


def solution(mesh):
    sizes = tuple(mesh.shape[axis] for axis in ("gx", "gy", "gz"))
    return jax.shard_map(
        functools.partial(shards, sizes),
        mesh=mesh,
        in_specs=(
            P(None, None, ("gx", "gy", "gz")),
            P(None, "gx", "gy", "gz"),
            P("gx", "gy", "gz"),
            P(),
            P(),
            P(("gx", "gy", "gz"), None),
            P(None, None, "gy", "gz"),
        ),
        out_specs=P(None, None, ("gx", "gy", "gz")),
        check_vma=False,
    )
```
